32 devices in a mesh: groups: 2 (over x), dom: 16 (over z, y, core).
Axes of the slice: x: 2, y: 2, z: 4, core: 2. Of those that a mesh axis runs over, the one named last changes fastest.
Arguments:
- particle_places: float32 [16, 3, 3072], P('groups', None, 'dom'), parts along dimension 0, may hold values from 0 to 48, as said below
- particle_speeds: float32 [16, 3, 3072], P('groups', None, 'dom'), parts along dimension 0, may hold values from -7 to 7
- thermal_targets: float32 [16], P('groups'), parts along dimension 0, may hold values from 0.5 to 2
- element_features: bfloat16 [6144, 128], P(('groups', 'dom')), parts along dimension 0, may hold values from -4 to 4
- swap_counterpart_slot: int32 [16], P('groups'), parts along dimension 0, may hold values from 0 to 7, as said below
- swap_approval_flags: int32 [16], P('groups'), parts along dimension 0, may hold values from 0 to 1, as said below
- initial_signal_projector: bfloat16 [128, 128], replicated, may hold values from -0.5 to 0.5
- initial_distance_filter: float32 [8, 128], replicated, may hold values from -2 to 2
- initial_directional_scales: float32 [128], replicated, may hold values from 0.5 to 1.5
- invariant_revision_matrix: bfloat16 [128, 128], replicated, may hold values from -0.5 to 0.5
- magnitude_revision_matrix: bfloat16 [128, 128], replicated, may hold values from -0.5 to 0.5
- later_signal_projector: bfloat16 [128, 128], replicated, may hold values from -0.5 to 0.5
- later_directional_scales: float32 [128], replicated, may hold values from 0.5 to 1.5
- push_output_matrix: float32 [128], replicated, may hold values from -0.5 to 0.5
Outputs:
- positions_new: float32 [16, 3, 3072], P('groups', None, 'dom'), parts along dimension 0
- velocities_new: float32 [16, 3, 3072], P('groups', None, 'dom'), parts along dimension 0
- forces_new: float32 [16, 3, 3072], P('groups', None, 'dom'), parts along dimension 0
The draws below stay inside these ranges and needn't reach their ends.
There are 2 independent parts, one for each index of `groups`. The reference program is written for one: setup_inputs(seed, part) draws one part's arguments, and reference() takes and returns one part's arrays. A program takes and returns all parts, laid end to end along the dimension named above; an argument that names none is the same for every part. Nothing has to cross between parts.
Inputs may be any that keep to these rules, and one draw needn't show every extreme that they name: `particle_places`: the atoms of cell k have x and y in [0, 1) and z in [k, k + 1). `swap_counterpart_slot`: an involution that pairs neighbouring replicas, either (0, 1), (2, 3), ... or (1, 2), (3, 4), ..., a replica left without a pair being its own partner. `swap_approval_flags`: equal for the two replicas of a pair, 0 for a replica that is its own partner.
All inputs are finite; a program needn't handle non-finite values.
Results may differ from the reference program's by a relative error of at most 0.012.
The reference program's roundings to bfloat16 on the way count: a program that leaves them out, or rounds other values in their place, can miss the bound.
Values may be sent and summed in bfloat16 or wider, within the bound.
A program may use at most 64 MiB of HBM per device.

```python
import math
import jax
import jax.numpy as jnp
from jax import lax

LADDER_RUNGS = 8
NA = 64
HC = 1
F = 128
K = 8
STEPS = 4
NC = 48
ATOMS = 3072


def draw_particle_places(key, part):
    spread = jax.random.uniform(jax.random.fold_in(key, 3), (LADDER_RUNGS, 3, ATOMS), jnp.float32)
    cell_rows = (jnp.arange(ATOMS) // NA).astype(jnp.float32)
    lifted = jnp.array([0.0, 0.0, 1.0], jnp.float32)[None, :, None] * cell_rows[None, None, :]
    return spread + lifted


def draw_particle_speeds(key, part):
    cell_frac = (jnp.arange(ATOMS) // NA).astype(jnp.float32) / NC
    drawn_base = jnp.clip(jax.random.normal(jax.random.fold_in(key, 5), (LADDER_RUNGS, 3, ATOMS), jnp.float32), -4.0, 4.0)
    return drawn_base * jnp.sqrt(1.0 + 2.0 * cell_frac)[None, None, :]


def swap_table(key, part):
    coin_parity = jax.random.randint(jax.random.fold_in(key, 7), (), 0, 2)
    parity = (coin_parity + jnp.asarray(part, jnp.int32)) % 2
    ladder_slot = jnp.arange(LADDER_RUNGS)
    paired = ladder_slot + 1 - 2 * ((ladder_slot + parity) % 2)
    exchange_mate = jnp.where((paired < 0) | (paired >= LADDER_RUNGS), ladder_slot, paired)
    coin_flips = jax.random.randint(jax.random.fold_in(key, 11), (LADDER_RUNGS,), 0, 2)
    coin_flips = jnp.where(ladder_slot == parity, 1, coin_flips)
    coin_flips = jnp.where(ladder_slot == LADDER_RUNGS - 2 - parity, 0, coin_flips)
    low_index = jnp.minimum(ladder_slot, exchange_mate)
    accepted = coin_flips[low_index]
    accepted = jnp.where(exchange_mate == ladder_slot, 0, accepted)
    return (exchange_mate.astype(jnp.int32), accepted.astype(jnp.int32))


def draw_swap_counterpart_slot(key, part):
    return swap_table(key, part)[0]


def draw_swap_approval_flags(key, part):
    return swap_table(key, part)[1]


def shard_levels(own_key, extent, cuts, least, largest):
    def one(position, blocks):
        draws = jax.random.uniform(jax.random.fold_in(jax.random.fold_in(own_key, 6), position), (blocks,), jnp.float32, least / len(cuts), largest / len(cuts))
        return jnp.repeat(jnp.exp(draws), extent[position] // blocks).reshape((-1,) + (1,) * (len(extent) - position - 1))

    factor_of = one(*cuts[0])
    for cut in cuts[1:]:
        factor_of = factor_of * one(*cut)
    return factor_of


def bell_draw(own_key, dims, width, reach, pieces=(), kind=jnp.bfloat16):
    values = jax.random.normal(own_key, dims, jnp.float32) * width
    if len(pieces) > 0:
        values = shard_levels(own_key, dims, pieces, -0.22, 0.18) * values
    return jnp.clip(values, min=-reach, max=reach).astype(kind)


def setup_inputs(seed: int = 0, part: int = 0) -> dict:
    key_of = jax.random.split(jax.random.key(seed), 15)
    part_splits = jax.random.split(jax.random.fold_in(key_of[14], part), 15)
    particle_places = draw_particle_places(jax.random.fold_in(jax.random.fold_in(key_of[14], part), 71), part)
    particle_speeds = draw_particle_speeds(jax.random.fold_in(jax.random.fold_in(key_of[14], part), 71), part)
    thermal_targets = jnp.clip(jnp.exp(jax.random.uniform(part_splits[2], (LADDER_RUNGS,), jnp.float32, math.log(0.5), math.log(2.0))), 0.5, 2.0)
    element_features = bell_draw(part_splits[3], (ATOMS, F), 1.0, 4.0, ((0, 16),))
    swap_counterpart_slot = draw_swap_counterpart_slot(jax.random.fold_in(jax.random.fold_in(key_of[14], part), 71), part)
    swap_approval_flags = draw_swap_approval_flags(jax.random.fold_in(jax.random.fold_in(key_of[14], part), 71), part)
    initial_signal_projector = bell_draw(key_of[6], (F, F), F ** -0.5, 0.5)
    initial_distance_filter = bell_draw(key_of[7], (K, F), K ** -0.5, 2.0, (), jnp.float32)
    initial_directional_scales = jnp.clip(jax.random.uniform(key_of[8], (F,), jnp.float32, 0.5, 1.5), 0.5, 1.5)
    invariant_revision_matrix = bell_draw(key_of[9], (F, F), F ** -0.5, 0.5)
    magnitude_revision_matrix = bell_draw(key_of[10], (F, F), F ** -0.5, 0.5)
    later_signal_projector = bell_draw(key_of[11], (F, F), F ** -0.5, 0.5)
    later_directional_scales = jnp.clip(jax.random.uniform(key_of[12], (F,), jnp.float32, 0.5, 1.5), 0.5, 1.5)
    push_output_matrix = bell_draw(key_of[13], (F,), F ** -0.5, 0.5, (), jnp.float32)
    return dict(particle_places=particle_places, particle_speeds=particle_speeds, thermal_targets=thermal_targets, element_features=element_features, swap_counterpart_slot=swap_counterpart_slot, swap_approval_flags=swap_approval_flags, initial_signal_projector=initial_signal_projector, initial_distance_filter=initial_distance_filter, initial_directional_scales=initial_directional_scales, invariant_revision_matrix=invariant_revision_matrix, magnitude_revision_matrix=magnitude_revision_matrix, later_signal_projector=later_signal_projector, later_directional_scales=later_directional_scales, push_output_matrix=push_output_matrix)


step_time = 0.05
motion_work_lower_limit = 1e-06

def radial_rows(own_coords, part_coords, basis_count):
    displacement = part_coords[:, :, :, None, :] - own_coords[:, :, :, :, None]
    squared = lax.optimization_barrier(jnp.sum(displacement * displacement, axis=1))
    envelope = jnp.where(squared < 1.0, (1.0 - squared) * (1.0 - squared), 0.0)
    vectors = jnp.moveaxis(displacement * envelope[:, None], 1, 3)
    if basis_count == 0:
        return vectors.astype(jnp.bfloat16)
    centers = jnp.arange(basis_count, dtype=jnp.float32) / (basis_count - 1)
    sharpness = 2.0 * (basis_count - 1) * (basis_count - 1)
    offset = squared[:, :, :, None, :] - centers[:, None]
    gaussians = jnp.exp(-sharpness * offset * offset) * envelope[:, :, :, None, :]
    return jnp.concatenate([gaussians, vectors], axis=3).astype(jnp.bfloat16)

def periodic_pad(source_array, width_atoms, along_axis):
    length = source_array.shape[along_axis]
    head_part = lax.slice_in_dim(source_array, length - width_atoms, length, axis=along_axis)
    tail_part = lax.slice_in_dim(source_array, 0, width_atoms, axis=along_axis)
    return jnp.concatenate([head_part, source_array, tail_part], axis=along_axis)

def force_field(location_triples, element_features, first_table, initial_distance_filter, initial_directional_scales, invariant_revision_matrix, magnitude_revision_matrix, later_signal_projector, later_directional_scales, push_output_matrix):
    replicas = location_triples.shape[0]
    cell_total = location_triples.shape[2] // NA
    channels = invariant_revision_matrix.shape[0]
    basis_count = initial_distance_filter.shape[0]
    reach_atoms = (2 * HC + 1) * NA
    padded = periodic_pad(location_triples, HC * NA, 2)
    cell_number = jnp.arange(padded.shape[2], dtype=jnp.int32) // NA - HC
    wrap_shift = (jnp.where(cell_number < 0, -1.0, 0.0) + jnp.where(cell_number >= cell_total, 1.0, 0.0)) * cell_total
    axis_mask = jnp.array([0.0, 0.0, 1.0], jnp.float32)
    near_coords = padded + axis_mask[None, :, None] * wrap_shift[None, None, :]

    def windows(cell_index):
        own_coords = lax.dynamic_slice_in_dim(near_coords, (cell_index + HC) * NA, NA, 2)
        part_coords = lax.dynamic_slice_in_dim(near_coords, cell_index * NA, reach_atoms, 2)
        return (own_coords[:, :, None], part_coords[:, :, None])

    def layer_one(cell_index):
        own_coords, part_coords = windows(cell_index)
        single_row_count = lax.optimization_barrier(radial_rows(own_coords, part_coords, basis_count)).astype(jnp.float32)
        exchange_mate = lax.dynamic_slice_in_dim(first_table, cell_index * NA, reach_atoms, 0).astype(jnp.float32)
        reduced_sum = jnp.einsum('rcaxb,bf->rcaxf', single_row_count, exchange_mate, precision=lax.Precision.HIGHEST)[:, 0]
        scalar = lax.optimization_barrier(jnp.sum(reduced_sum[:, :, :basis_count] * initial_distance_filter, axis=2))
        vector_one = reduced_sum[:, :, basis_count:] * initial_directional_scales
        norm_square = lax.optimization_barrier(jnp.sum(vector_one * vector_one, axis=2))
        update = jnp.dot(scalar.astype(jnp.bfloat16).reshape(-1, channels), invariant_revision_matrix, preferred_element_type=jnp.float32)
        update = update + jnp.dot(norm_square.astype(jnp.bfloat16).reshape(-1, channels), magnitude_revision_matrix, preferred_element_type=jnp.float32)
        self_rows = lax.dynamic_slice_in_dim(element_features, cell_index * NA, NA, 0).astype(jnp.float32)
        hidden = (self_rows[None] + jax.nn.silu(update).reshape(replicas, NA, channels)).astype(jnp.bfloat16)
        return (hidden, vector_one)
    cell_list = jnp.arange(cell_total, dtype=jnp.int32)
    hidden_all, vector_all = lax.map(layer_one, cell_list)
    hidden_rows = jnp.moveaxis(hidden_all, 0, 1).reshape(replicas * cell_total * NA, channels)
    second = jnp.dot(hidden_rows, later_signal_projector, preferred_element_type=jnp.float32).astype(jnp.bfloat16)
    second_table = periodic_pad(second.reshape(replicas, cell_total * NA, channels), HC * NA, 1)

    def layer_two(cell_index):
        own_coords, part_coords = windows(cell_index)
        rows_two = lax.optimization_barrier(radial_rows(own_coords, part_coords, 0)).astype(jnp.float32)
        exchange_mate = lax.dynamic_slice_in_dim(second_table, cell_index * NA, reach_atoms, 1).astype(jnp.float32)
        reduced_sum = jnp.einsum('rcaxb,rbf->rcaxf', rows_two, exchange_mate, precision=lax.Precision.HIGHEST)[:, 0]
        total = vector_all[cell_index] + reduced_sum * later_directional_scales
        return lax.optimization_barrier(jnp.sum(total * push_output_matrix, axis=3))
    force_cells = lax.map(layer_two, cell_list)
    return jnp.transpose(force_cells, (1, 3, 0, 2)).reshape(replicas, 3, cell_total * NA)

def reference(particle_places, particle_speeds, thermal_targets, element_features, swap_counterpart_slot, swap_approval_flags, initial_signal_projector, initial_distance_filter, initial_directional_scales, invariant_revision_matrix, magnitude_revision_matrix, later_signal_projector, later_directional_scales, push_output_matrix):
    particle_number_overall = particle_places.shape[2]
    first_table = periodic_pad(jnp.dot(element_features, initial_signal_projector, preferred_element_type=jnp.float32).astype(jnp.bfloat16), HC * NA, 0)

    def evaluate(location_triples):
        return force_field(location_triples, element_features, first_table, initial_distance_filter, initial_directional_scales, invariant_revision_matrix, magnitude_revision_matrix, later_signal_projector, later_directional_scales, push_output_matrix)
    location_triples = particle_places
    speed_entry = particle_speeds
    present_push = evaluate(location_triples)
    for step_index in range(STEPS):
        half_velocity = speed_entry + 0.5 * step_time * present_push
        location_triples = location_triples + step_time * half_velocity
        present_push = evaluate(location_triples)
        speed_entry = half_velocity + 0.5 * step_time * present_push
        motion_work_amount = lax.optimization_barrier(jnp.sum(speed_entry * speed_entry, axis=(1, 2)))
        stretch_multiplier = jnp.sqrt(thermal_targets / (motion_work_amount / (3.0 * particle_number_overall) + motion_work_lower_limit))
        speed_entry = speed_entry * stretch_multiplier[:, None, None]
    ladder_slot = jnp.arange(thermal_targets.shape[0], dtype=jnp.int32)
    source = jnp.where(swap_approval_flags > 0, swap_counterpart_slot, ladder_slot)
    selected_entries = (source[:, None] == ladder_slot[None, :]).astype(jnp.float32)

    def select_entries(values):
        return lax.optimization_barrier(jnp.sum(selected_entries[:, :, None, None] * values[None], axis=1))
    thermal_ratio = jnp.sqrt(thermal_targets / lax.optimization_barrier(jnp.sum(selected_entries * thermal_targets[None, :], axis=1)))
    atom_cell = (jnp.arange(particle_number_overall, dtype=jnp.int32) // NA).astype(jnp.float32)
    cell_floor = jnp.array([0.0, 0.0, 1.0], jnp.float32)[:, None] * atom_cell[None, :]
    return (select_entries(location_triples) - cell_floor[None], select_entries(speed_entry) * thermal_ratio[:, None, None], select_entries(present_push))
```

```python
import functools
import math

import jax
import jax.numpy as jnp
from jax import lax
from jax.experimental import pallas as pl
from jax.experimental.pallas import tpu as pltpu
from jax.sharding import PartitionSpec as P

NA = 64
STEPS = 4
LANES = 128
CHUNK = 16
HALO = 2
SPLITS = 3
LOG2E = math.log2(math.e)

step_time = 0.05
motion_work_lower_limit = 1e-06

F32 = jnp.float32
BF16 = jnp.bfloat16
MESH = pl.DeviceIdType.MESH


def split_bf16(values):
    high = values.astype(BF16)
    low = (values - high.astype(F32)).astype(BF16)
    return high, low


def weight_rows(weights):
    high, low = split_bf16(weights)
    high, low = high.astype(F32), low.astype(F32)
    row = lax.broadcasted_iota(jnp.int32, (16, weights.shape[1]), 0)
    return jnp.where(row == 0, high, jnp.where(row == 1, low, 0.0)).astype(BF16)


def swap_halves(values):
    return pltpu.roll(values, NA, 1)


def kernel(
    n, replicas, cells, parts,
    places, speeds, targets, slots, flags, features,
    projector, radial_filter, scales_one, invariant, magnitude, later_projector, scales_two, push,
    places_out, speeds_out, forces_out,
    own_places, own_speeds, feats, w_project, w_filter, w_scale_one, w_invariant, w_magnitude,
    w_later, w_scale_two, w_push,
    place_halo, table_one, table_vec, feat_t, mix, later_t, scale_sq, read_two, s_one, selector,
    state_x, state_v, state_g, cols, xb, gauss, vecs, mixed,
    vg_send, vg_recv, kin_send, kin_recv,
    load_sem, init_send_sem, init_recv_sem, vg_send_sem, vg_recv_sem, kin_send_sem, kin_recv_sem,
):
    me = lax.axis_index("dom")
    left = lax.rem(me + n - 1, n)
    right = lax.rem(me + 1, n)
    own = cells * NA
    edge = HALO * NA
    ext = cells + 2 * HALO
    inner = cells + 2
    wide = state_x.shape[3]
    group = replicas // parts
    lanes = group * NA
    tiles = lanes // LANES
    channels = features.shape[1]
    basis = radial_filter.shape[0]
    near = 3 * NA

    barrier = pltpu.get_barrier_semaphore()

    def greet(d, carry):
        pl.semaphore_signal(barrier, inc=1, device_id={"dom": lax.rem(me + d, n)}, device_id_type=MESH)
        return carry

    loads = [
        (features, feats.at[pl.ds(edge, own)]),
        (projector, w_project),
        (places, own_places),
        (speeds, own_speeds),
        (radial_filter, w_filter),
        (scales_one, w_scale_one),
        (invariant, w_invariant),
        (magnitude, w_magnitude),
        (later_projector, w_later),
        (scales_two, w_scale_two),
        (push, w_push),
    ]
    loads = [pltpu.make_async_copy(src, dst, load_sem.at[i]) for i, (src, dst) in enumerate(loads)]
    for load in loads:
        load.start()
    lax.fori_loop(1, n, greet, 0)

    def remote(src, dst, send_sem, recv_sem, to):
        return pltpu.make_async_remote_copy(
            src_ref=src, dst_ref=dst, send_sem=send_sem, recv_sem=recv_sem,
            device_id={"dom": to}, device_id_type=MESH,
        )

    first = [
        remote(places, place_halo.at[1], init_send_sem.at[0], init_recv_sem.at[0], left),
        remote(places, place_halo.at[0], init_send_sem.at[1], init_recv_sem.at[1], right),
        remote(
            features.at[pl.ds(0, edge)], feats.at[pl.ds(edge + own, edge)],
            init_send_sem.at[2], init_recv_sem.at[2], left,
        ),
        remote(
            features.at[pl.ds(own - edge, edge)], feats.at[pl.ds(0, edge)],
            init_send_sem.at[3], init_recv_sem.at[3], right,
        ),
    ]
    pl.semaphore_wait(barrier, n - 1)
    for copy in first:
        copy.start()
    for load in loads:
        load.wait()

    half_lane = lax.broadcasted_iota(jnp.int32, (1, LANES), 1) < NA
    member_row = lax.broadcasted_iota(jnp.int32, (group, 1), 0)

    def flip(values):
        return values.astype(F32).T

    def column(row):
        return jnp.broadcast_to(row.T[:, 0:1], (channels, LANES))

    offset = lax.broadcasted_iota(jnp.int32, (basis, channels), 0).astype(F32) - 0.5 * (basis - 1)
    filters = (w_filter[...] * jnp.exp(-2.0 * offset * offset)).T
    push_row = w_push[...]
    w_one = weight_rows(w_scale_one[...] * push_row)
    read_two[...] = weight_rows(w_scale_two[...] * push_row)
    scale_row = jnp.broadcast_to(w_scale_one[...] * w_scale_one[...], (8, channels))
    scale_sq[...] = column(scale_row)
    mix[:, 0:channels] = (0.5 * flip(w_invariant[...])).astype(BF16)
    mix[:, channels:2 * channels] = (0.5 * flip(w_magnitude[...])).astype(BF16)
    later_t[...] = flip(w_later[...]).astype(BF16)

    k_row = lax.broadcasted_iota(jnp.int32, (LANES, lanes), 0)
    k_lane = lax.broadcasted_iota(jnp.int32, (LANES, lanes), 1)
    for d in range(3):
        base = d * SPLITS * group
        inside = (k_row >= base) & (k_row < base + SPLITS * group)
        chosen = inside & ((k_row - base) % group == k_lane // NA)
        selector[d] = jnp.where(chosen, 1.0, 0.0).astype(BF16)
    for p in range(parts):
        for i in range(inner):
            for d in range(3):
                vecs[p, i, d, near:, :] = jnp.zeros((4 * NA - near, lanes), BF16)
    feats[ext * NA:, :] = jnp.zeros((wide - ext * NA, channels), BF16)

    total = cells * n
    floor_own = (me * cells).astype(F32)
    floor_left = (me * cells + jnp.where(me == 0, total, 0)).astype(F32)
    floor_right = (me * cells - jnp.where(me == n - 1, total, 0)).astype(F32)
    lift = [0.0, 0.0, 1.0]
    tail = jnp.zeros((group, wide - ext * NA), F32)
    for p in range(parts):
        members = slice(p * group, (p + 1) * group)
        for d in range(3):
            state_v[p, d] = jnp.concatenate(
                [jnp.zeros((group, edge), F32), own_speeds[d, members, :], jnp.zeros((group, edge), F32), tail],
                axis=1,
            )
            state_g[p, d] = jnp.zeros((group, wide), F32)

    for copy in first:
        copy.wait()

    for p in range(parts):
        members = slice(p * group, (p + 1) * group)
        for d in range(3):
            state_x[p, d] = jnp.concatenate(
                [
                    place_halo[0, d, members, own - edge:] - lift[d] * floor_left,
                    own_places[d, members, :] - lift[d] * floor_own,
                    place_halo[1, d, members, :edge] - lift[d] * floor_right,
                    tail,
                ],
                axis=1,
            )

    signals = jnp.dot(feats[...], w_project[...], preferred_element_type=F32).astype(BF16)
    signal_tiles = [flip(signals[at:at + LANES]) for at in range(0, wide, LANES)]
    feat_tiles = [flip(feats[at:at + LANES, :]) for at in range(0, wide, LANES)]

    def double(tile_list, e):
        tile = tile_list[e // 2]
        other = swap_halves(tile)
        return jnp.where(half_lane, tile, other) if e % 2 == 0 else jnp.where(half_lane, other, tile)

    doubles = [double(signal_tiles, e) for e in range(ext)]
    flat_signals = jnp.concatenate(signal_tiles, axis=1).astype(BF16)
    out = jnp.dot(w_one, flat_signals, preferred_element_type=F32)
    s_one[...] = out[0:1] + out[1:2]
    for i in range(inner):
        feat_t[i] = double(feat_tiles, i + 1)
        pair = jnp.where(half_lane, doubles[i], doubles[i + 1])
        table_vec[i, :, 0:LANES] = pair.astype(BF16)
        table_vec[i, :, LANES:2 * LANES] = jnp.where(half_lane, doubles[i + 2], 0.0).astype(BF16)
        for k in range(basis):
            col = jnp.broadcast_to(filters[:, k:k + 1], (channels, LANES))
            table_one[i, :, k * LANES:(k + 1) * LANES] = (pair * col).astype(BF16)
            if k % 2 == 1:
                both = jnp.where(half_lane, jnp.broadcast_to(filters[:, k - 1:k], (channels, LANES)), col)
                at = basis * LANES + (k // 2) * LANES
                table_one[i, :, at:at + LANES] = (doubles[i + 2] * both).astype(BF16)

    replica_row = lax.broadcasted_iota(jnp.int32, (replicas, 1), 0)
    diagonal = (
        lax.broadcasted_iota(jnp.int32, (group, LANES), 0)
        == lax.broadcasted_iota(jnp.int32, (group, LANES), 1)
    )
    target = jnp.zeros((replicas, 1), F32)
    source = jnp.zeros((replicas, 1), jnp.int32)
    for r in range(replicas):
        target = jnp.where(replica_row == r, targets[r], target)
        source = jnp.where(replica_row == r, jnp.where(flags[r] > 0, slots[r], r), source)

    def spread_row(tile_list, e):
        tile = tile_list[e // 2]
        other = swap_halves(tile)
        first_half, second_half = (tile, other) if e % 2 == 0 else (other, tile)
        return [
            jnp.where(half_lane, first_half[2 * m:2 * m + 1], second_half[2 * m + 1:2 * m + 2])
            for m in range(tiles)
        ]

    def gather_rows(values, odd):
        result = None
        for r in range(group):
            tile = values[:, (r // 2) * LANES:(r // 2 + 1) * LANES]
            if (r % 2 == 1) != odd:
                tile = swap_halves(tile)
            result = tile if result is None else jnp.where(member_row == r, tile, result)
        return jnp.broadcast_to(result, (group, LANES))

    def pairs(p, i, place_tiles):
        e = i + 1
        mine = [
            jnp.broadcast_to(jnp.concatenate(spread_row(place_tiles[d], e), axis=1), (CHUNK, lanes))
            for d in range(3)
        ]
        for at in range(0, near, CHUNK):
            row = i * NA + at
            dx, dy, dz = [xb[p, d, row:row + CHUNK, :] - mine[d] for d in range(3)]
            squared = dx * dx + dy * dy + dz * dz
            inside = jnp.maximum(1.0 - squared, 0.0)
            envelope = inside * inside
            for d, step in enumerate((dx, dy, dz)):
                vecs[p, i, d, at:at + CHUNK, :] = (step * envelope).astype(BF16)
            centered = 0.5 - inside
            value = jnp.exp2((centered * (centered + 1.0)) * (-98.0 * LOG2E)) * envelope
            ratio = jnp.exp2(centered * (28.0 * LOG2E))
            for k in range(basis):
                if at < 2 * NA:
                    to = k * LANES + at
                else:
                    to = basis * LANES + k * NA + at - 2 * NA
                gauss[p, i, to:to + CHUNK, :] = value.astype(BF16)
                if k + 1 < basis:
                    value = value * ratio

    def dense(p, i):
        scalar = jnp.dot(table_one[i], gauss[p, i], preferred_element_type=F32)
        mixed[p, i, 0:channels, :] = scalar.astype(BF16)
        norm = None
        for d in range(3):
            vec = jnp.dot(table_vec[i], vecs[p, i, d], preferred_element_type=F32)
            norm = vec * vec if norm is None else norm + vec * vec
        norm = norm * jnp.concatenate([scale_sq[...]] * tiles, axis=1)
        mixed[p, i, channels:, :] = norm.astype(BF16)
        half = jnp.dot(mix[...], mixed[p, i], preferred_element_type=F32)
        hidden = half * jnp.tanh(half) + half + jnp.concatenate([feat_t[i]] * tiles, axis=1)
        second = jnp.dot(later_t[...], hidden.astype(BF16), preferred_element_type=F32).astype(BF16)
        out = jnp.dot(read_two[...], second, preferred_element_type=F32)
        return out[0:1] + out[1:2]

    def force(p, e, strengths):
        window = strengths[:, (e - 1) * NA:(e + 3) * NA]
        high, low = split_bf16(window)
        stacked = jnp.concatenate([high.astype(F32), low.astype(F32)], axis=0)
        stacked = jnp.concatenate([stacked] * (16 // (2 * group)), axis=0).astype(BF16)
        result = []
        for d in range(3):
            out = jnp.dot(stacked, vecs[p, e - 1, d], preferred_element_type=F32)
            result.append(gather_rows(out[:group] + out[group:2 * group], e % 2 == 1))
        return result

    def is_moving(t):
        return jnp.where(t > 0, 1.0, 0.0).astype(F32)

    def vg_copies(t, p):
        return [
            remote(vg_send.at[t, p, 0], vg_recv.at[t, p, 1], vg_send_sem.at[t, p, 0], vg_recv_sem.at[t, p, 0], left),
            remote(vg_send.at[t, p, 1], vg_recv.at[t, p, 0], vg_send_sem.at[t, p, 1], vg_recv_sem.at[t, p, 1], right),
        ]

    def advance(t, p):
        moving = is_moving(t)
        place_tiles = []
        stack = []
        for d in range(3):
            half = state_v[p, d] + (0.5 * step_time) * state_g[p, d]
            x = state_x[p, d] + (moving * step_time) * half
            state_v[p, d] = half
            state_x[p, d] = x
            place_tiles.append([x[:, at:at + LANES] for at in range(0, wide, LANES)])
            rest = x
            for s in range(SPLITS):
                piece = rest.astype(BF16).astype(F32)
                rest = rest - piece
                stack.append(piece)
        stack.append(jnp.zeros((LANES - 3 * SPLITS * group, wide), F32))
        tall = jnp.concatenate(stack, axis=0)
        for at in range(0, wide, LANES):
            cols[p, at:at + LANES, :] = tall[:, at:at + LANES].T.astype(BF16)
        for d in range(3):
            xb[p, d] = jnp.dot(cols[p, 0:ext * NA, :], selector[d], preferred_element_type=F32)
        flats = []
        for i in range(inner):
            pairs(p, i, place_tiles)
            flats.append(dense(p, i))
        strengths = []
        for at in range(0, wide // NA, 2):
            even, odd = [
                gather_rows(flats[e - 1], e % 2 == 1) if 1 <= e <= inner else jnp.zeros((group, LANES), F32)
                for e in (at, at + 1)
            ]
            strengths.append(jnp.where(half_lane, even, odd))
        strengths = jnp.concatenate(strengths, axis=1) + s_one[...]
        pushes = [force(p, e, strengths) for e in range(HALO, HALO + cells)]
        kinetic = jnp.zeros((group, 1), F32)
        for d in range(3):
            joined = []
            for c in range(0, cells, 2):
                even = pushes[c][d]
                odd = pushes[c + 1][d] if c + 1 < cells else jnp.zeros((group, LANES), F32)
                joined.append(jnp.where(half_lane, even, odd))
            g = jnp.concatenate(joined, axis=1)[:, :own]
            v = state_v[p, d, :, edge:edge + own] + (moving * (0.5 * step_time)) * g
            vg_send[t, p, 0, d] = jnp.concatenate([v[:, :edge], g[:, :edge]], axis=1)
            vg_send[t, p, 1, d] = jnp.concatenate([v[:, own - edge:], g[:, own - edge:]], axis=1)
            kinetic = kinetic + jnp.sum(v * v, axis=1, keepdims=True)
            state_v[p, d, :, edge:edge + own] = v
            state_g[p, d, :, edge:edge + own] = g
        across = jnp.sum(jnp.where(diagonal, kinetic, 0.0), axis=0, keepdims=True)
        kin_send[t, p] = across
        kin_recv[t, p, n - 1] = across

        def spread(d, inner_carry):
            remote(
                kin_send.at[t, p], kin_recv.at[t, p, d - 1], kin_send_sem.at[t, p],
                kin_recv_sem.at[t, p], lax.rem(me + d, n),
            ).start()
            return inner_carry

        for copy in vg_copies(t, p):
            copy.start()
        lax.fori_loop(1, n, spread, 0)

    def finish(t, p):
        everything = kin_recv.at[t, p, pl.ds(0, n - 1)]
        for copy in vg_copies(t, p):
            copy.wait()
        pltpu.make_async_copy(everything, everything, kin_send_sem.at[t, p]).wait()
        pltpu.make_async_copy(everything, everything, kin_recv_sem.at[t, p]).wait()
        collected = jnp.sum(kin_recv[t, p], axis=0)
        gathered = jnp.sum(jnp.where(diagonal, collected, 0.0), axis=1, keepdims=True)
        goal = target[p * group:(p + 1) * group]
        stretch = jnp.sqrt(goal / (gathered / (3.0 * own * n) + motion_work_lower_limit))
        stretch = jnp.where(t > 0, stretch, 1.0)
        rest = jnp.zeros((group, wide - ext * NA), F32)
        for d in range(3):
            from_left, from_right = vg_recv[t, p, 0, d], vg_recv[t, p, 1, d]
            state_v[p, d] = stretch * jnp.concatenate(
                [from_left[:, :edge], state_v[p, d, :, edge:edge + own], from_right[:, :edge], rest], axis=1
            )
            state_g[p, d, :, 0:edge] = from_left[:, edge:]
            state_g[p, d, :, edge + own:2 * edge + own] = from_right[:, edge:]

    def step(t, carry):
        for p in range(parts):
            pl.when(t > 0)(functools.partial(finish, t - 1, p))
            advance(t, p)
        return carry

    lax.fori_loop(0, STEPS + 1, step, 0)
    for p in range(parts):
        finish(STEPS, p)

    def pick(values):
        result = jnp.zeros_like(values)
        for r in range(replicas):
            result = jnp.where(source == r, values[r:r + 1], result)
        return result

    def whole(state, d):
        return jnp.concatenate([state[p, d, :, edge:edge + own] for p in range(parts)], axis=0)

    heat = jnp.sqrt(target / pick(target))
    floor = (lax.broadcasted_iota(jnp.int32, (1, own), 1) // NA).astype(F32)
    for d in range(3):
        x = pick(whole(state_x, d))
        if d == 2:
            x = x - floor
        places_out[d] = x
        speeds_out[d] = pick(whole(state_v, d)) * heat
        forces_out[d] = pick(whole(state_g, d))


def on_device(
    particle_places,
    particle_speeds,
    thermal_targets,
    element_features,
    swap_counterpart_slot,
    swap_approval_flags,
    initial_signal_projector,
    initial_distance_filter,
    initial_directional_scales,
    invariant_revision_matrix,
    magnitude_revision_matrix,
    later_signal_projector,
    later_directional_scales,
    push_output_matrix,
):
    n = lax.axis_size("dom")
    replicas, _, own = particle_places.shape
    cells = own // NA
    channels = element_features.shape[1]
    ext = cells + 2 * HALO
    inner = cells + 2
    edge = HALO * NA
    wide = -(-ext * NA // LANES) * LANES
    rounds = STEPS + 1
    group = 4
    parts = replicas // group
    lanes = group * NA
    basis = initial_distance_filter.shape[0]
    depth = basis * 3 * NA
    vmem = pl.BlockSpec(memory_space=pltpu.VMEM)
    smem = pl.BlockSpec(memory_space=pltpu.SMEM)
    outside = pl.BlockSpec(memory_space=pl.ANY)
    out = jax.ShapeDtypeStruct((3, replicas, own), F32)
    results = pl.pallas_call(
        functools.partial(kernel, n, replicas, cells, parts),
        out_shape=(out, out, out),
        in_specs=[outside, outside, smem, smem, smem] + [outside] * 9,
        out_specs=(vmem, vmem, vmem),
        scratch_shapes=[
            pltpu.VMEM((3, replicas, own), F32),
            pltpu.VMEM((3, replicas, own), F32),
            pltpu.VMEM((wide, channels), BF16),
            pltpu.VMEM((channels, channels), BF16),
            pltpu.VMEM((basis, channels), F32),
            pltpu.VMEM((1, channels), F32),
            pltpu.VMEM((channels, channels), BF16),
            pltpu.VMEM((channels, channels), BF16),
            pltpu.VMEM((channels, channels), BF16),
            pltpu.VMEM((1, channels), F32),
            pltpu.VMEM((1, channels), F32),
            pltpu.VMEM((2, 3, replicas, own), F32),
            pltpu.VMEM((inner, channels, depth), BF16),
            pltpu.VMEM((inner, channels, 4 * NA), BF16),
            pltpu.VMEM((inner, channels, LANES), F32),
            pltpu.VMEM((channels, 2 * channels), BF16),
            pltpu.VMEM((channels, channels), BF16),
            pltpu.VMEM((channels, LANES), F32),
            pltpu.VMEM((16, channels), BF16),
            pltpu.VMEM((1, wide), F32),
            pltpu.VMEM((3, LANES, lanes), BF16),
            pltpu.VMEM((parts, 3, group, wide), F32),
            pltpu.VMEM((parts, 3, group, wide), F32),
            pltpu.VMEM((parts, 3, group, wide), F32),
            pltpu.VMEM((parts, wide, LANES), BF16),
            pltpu.VMEM((parts, 3, ext * NA, lanes), F32),
            pltpu.VMEM((parts, inner, depth, lanes), BF16),
            pltpu.VMEM((parts, inner, 3, 4 * NA, lanes), BF16),
            pltpu.VMEM((parts, inner, 2 * channels, lanes), BF16),
            pltpu.VMEM((rounds, parts, 2, 3, group, 2 * edge), F32),
            pltpu.VMEM((rounds, parts, 2, 3, group, 2 * edge), F32),
            pltpu.VMEM((rounds, parts, 1, LANES), F32),
            pltpu.VMEM((rounds, parts, n, 1, LANES), F32),
            pltpu.SemaphoreType.DMA((11,)),
            pltpu.SemaphoreType.DMA((4,)),
            pltpu.SemaphoreType.DMA((4,)),
            pltpu.SemaphoreType.DMA((rounds, parts, 2)),
            pltpu.SemaphoreType.DMA((rounds, parts, 2)),
            pltpu.SemaphoreType.DMA((rounds, parts)),
            pltpu.SemaphoreType.DMA((rounds, parts)),
        ],
        compiler_params=pltpu.CompilerParams(
            collective_id=0, has_side_effects=True, vmem_limit_bytes=63 * 1024 * 1024
        ),
    )(
        jnp.transpose(particle_places, (1, 0, 2)),
        jnp.transpose(particle_speeds, (1, 0, 2)),
        thermal_targets,
        swap_counterpart_slot,
        swap_approval_flags,
        element_features,
        initial_signal_projector,
        initial_distance_filter,
        initial_directional_scales.reshape(1, -1),
        invariant_revision_matrix,
        magnitude_revision_matrix,
        later_signal_projector,
        later_directional_scales.reshape(1, -1),
        push_output_matrix.reshape(1, -1),
    )
    return tuple(jnp.transpose(result, (1, 0, 2)) for result in results)
def solution(mesh):
    along = P("groups", None, "dom")
    return jax.shard_map(
        on_device,
        mesh=mesh,
        in_specs=(
            along,
            along,
            P("groups"),
            P(("groups", "dom"), None),
            P("groups"),
            P("groups"),
            P(),
            P(),
            P(),
            P(),
            P(),
            P(),
            P(),
            P(),
        ),
        out_specs=(along, along, along),
        check_vma=False,
    )
```

```python
import functools
import math

import jax
import jax.numpy as jnp
from jax import lax
from jax.experimental import pallas as pl
from jax.experimental.pallas import tpu as pltpu
from jax.sharding import PartitionSpec as P

NA = 64
STEPS = 4
LANES = 128
CHUNK = 16
HALO = 2
SPLITS = 3
TERMS = 24
LOG2E = math.log2(math.e)

step_time = 0.05
motion_work_lower_limit = 1e-06

F32 = jnp.float32
BF16 = jnp.bfloat16
MESH = pl.DeviceIdType.MESH


def split_bf16(values):
    high = values.astype(BF16)
    low = (values - high.astype(F32)).astype(BF16)
    return high, low


def weight_rows(weights):
    high, low = split_bf16(weights)
    high, low = high.astype(F32), low.astype(F32)
    row = lax.broadcasted_iota(jnp.int32, (16, weights.shape[1]), 0)
    return jnp.where(row == 0, high, jnp.where(row == 1, low, 0.0)).astype(BF16)


def swap_halves(values):
    return pltpu.roll(values, NA, 1)


def kernel(
    n, replicas, cells, parts,
    places, speeds, targets, slots, flags, features,
    projector, radial_filter, scales_one, invariant, magnitude, later_projector, scales_two, push,
    places_out, speeds_out, forces_out,
    own_places, own_speeds, feats, w_project, w_filter, w_scale_one, w_invariant, w_magnitude,
    w_later, w_scale_two, w_push,
    place_halo, table_one, table_vec, feat_t, mix, later_t, scale_sq, read_two, s_one, selector,
    state_x, state_v, state_g, cols, xb, mine, near_w, apart, gauss, vecs, mixed, flats, pushes,
    vg_send, vg_recv, kin_send, kin_recv,
    load_sem, init_send_sem, init_recv_sem, vg_send_sem, vg_recv_sem, kin_send_sem, kin_recv_sem,
):
    me = lax.axis_index("dom")
    left = lax.rem(me + n - 1, n)
    right = lax.rem(me + 1, n)
    own = cells * NA
    edge = HALO * NA
    ext = cells + 2 * HALO
    inner = cells + 2
    wide = state_x.shape[3]
    group = replicas // parts
    lanes = group * NA
    tiles = lanes // LANES
    channels = features.shape[1]
    basis = radial_filter.shape[0]
    near = 3 * NA

    barrier = pltpu.get_barrier_semaphore()

    def greet(d, carry):
        pl.semaphore_signal(barrier, inc=1, device_id={"dom": lax.rem(me + d, n)}, device_id_type=MESH)
        return carry

    loads = [
        (features, feats.at[pl.ds(edge, own)]),
        (projector, w_project),
        (places, own_places),
        (speeds, own_speeds),
        (radial_filter, w_filter),
        (scales_one, w_scale_one),
        (invariant, w_invariant),
        (magnitude, w_magnitude),
        (later_projector, w_later),
        (scales_two, w_scale_two),
        (push, w_push),
    ]
    loads = [pltpu.make_async_copy(src, dst, load_sem.at[i]) for i, (src, dst) in enumerate(loads)]
    for load in loads:
        load.start()
    lax.fori_loop(1, n, greet, 0)

    def remote(src, dst, send_sem, recv_sem, to):
        return pltpu.make_async_remote_copy(
            src_ref=src, dst_ref=dst, send_sem=send_sem, recv_sem=recv_sem,
            device_id={"dom": to}, device_id_type=MESH,
        )

    first = [
        remote(places, place_halo.at[1], init_send_sem.at[0], init_recv_sem.at[0], left),
        remote(places, place_halo.at[0], init_send_sem.at[1], init_recv_sem.at[1], right),
        remote(
            features.at[pl.ds(0, edge)], feats.at[pl.ds(edge + own, edge)],
            init_send_sem.at[2], init_recv_sem.at[2], left,
        ),
        remote(
            features.at[pl.ds(own - edge, edge)], feats.at[pl.ds(0, edge)],
            init_send_sem.at[3], init_recv_sem.at[3], right,
        ),
    ]
    pl.semaphore_wait(barrier, n - 1)
    for copy in first:
        copy.start()
    for load in loads:
        load.wait()

    half_lane = lax.broadcasted_iota(jnp.int32, (1, LANES), 1) < NA
    member_row = lax.broadcasted_iota(jnp.int32, (group, 1), 0)

    def flip(values):
        return values.astype(F32).T

    def column(row):
        return jnp.broadcast_to(row.T[:, 0:1], (channels, LANES))

    offset = lax.broadcasted_iota(jnp.int32, (basis, channels), 0).astype(F32) - 0.5 * (basis - 1)
    filters = (w_filter[...] * jnp.exp(-2.0 * offset * offset)).T
    push_row = w_push[...]
    w_one = weight_rows(w_scale_one[...] * push_row)
    read_two[...] = weight_rows(w_scale_two[...] * push_row)
    scale_row = jnp.broadcast_to(w_scale_one[...] * w_scale_one[...], (8, channels))
    scale_sq[...] = column(scale_row)
    mix[:, 0:channels] = (0.5 * flip(w_invariant[...])).astype(BF16)
    mix[:, channels:2 * channels] = (0.5 * flip(w_magnitude[...])).astype(BF16)
    later_t[...] = flip(w_later[...]).astype(BF16)

    k_row = lax.broadcasted_iota(jnp.int32, (LANES, lanes), 0)
    k_lane = lax.broadcasted_iota(jnp.int32, (LANES, lanes), 1)
    for d in range(3):
        base = d * SPLITS * group
        inside = (k_row >= base) & (k_row < base + SPLITS * group)
        chosen = inside & ((k_row - base) % group == k_lane // NA)
        selector[d] = jnp.where(chosen, 1.0, 0.0).astype(BF16)
    for p in range(parts):
        for i in range(inner):
            for d in range(3):
                vecs[p, i, d, near:, :] = jnp.zeros((4 * NA - near, lanes), BF16)
            near_w[p, i, TERMS * group:, :] = jnp.zeros((LANES - TERMS * group, lanes), BF16)
    feats[ext * NA:, :] = jnp.zeros((wide - ext * NA, channels), BF16)

    total = cells * n
    floor_own = (me * cells).astype(F32)
    floor_left = (me * cells + jnp.where(me == 0, total, 0)).astype(F32)
    floor_right = (me * cells - jnp.where(me == n - 1, total, 0)).astype(F32)
    lift = [0.0, 0.0, 1.0]
    tail = jnp.zeros((group, wide - ext * NA), F32)
    for p in range(parts):
        members = slice(p * group, (p + 1) * group)
        for d in range(3):
            state_v[p, d] = jnp.concatenate(
                [jnp.zeros((group, edge), F32), own_speeds[d, members, :], jnp.zeros((group, edge), F32), tail],
                axis=1,
            )
            state_g[p, d] = jnp.zeros((group, wide), F32)

    for copy in first:
        copy.wait()

    for p in range(parts):
        members = slice(p * group, (p + 1) * group)
        for d in range(3):
            state_x[p, d] = jnp.concatenate(
                [
                    place_halo[0, d, members, own - edge:] - lift[d] * floor_left,
                    own_places[d, members, :] - lift[d] * floor_own,
                    place_halo[1, d, members, :edge] - lift[d] * floor_right,
                    tail,
                ],
                axis=1,
            )

    signals = jnp.dot(feats[...], w_project[...], preferred_element_type=F32).astype(BF16)
    signal_tiles = [flip(signals[at:at + LANES]) for at in range(0, wide, LANES)]
    feat_tiles = [flip(feats[at:at + LANES, :]) for at in range(0, wide, LANES)]

    def double(tile_list, e):
        tile = tile_list[e // 2]
        other = swap_halves(tile)
        return jnp.where(half_lane, tile, other) if e % 2 == 0 else jnp.where(half_lane, other, tile)

    doubles = [double(signal_tiles, e) for e in range(ext)]
    flat_signals = jnp.concatenate(signal_tiles, axis=1).astype(BF16)
    out = jnp.dot(w_one, flat_signals, preferred_element_type=F32)
    s_one[:, 0:wide] = out[0:1] + out[1:2]
    s_one[:, wide:] = jnp.zeros((1, LANES), F32)
    for i in range(inner):
        feat_t[i] = double(feat_tiles, i + 1)
        pair = jnp.where(half_lane, doubles[i], doubles[i + 1])
        table_vec[i, :, 0:LANES] = pair.astype(BF16)
        table_vec[i, :, LANES:2 * LANES] = jnp.where(half_lane, doubles[i + 2], 0.0).astype(BF16)
        for k in range(basis):
            col = jnp.broadcast_to(filters[:, k:k + 1], (channels, LANES))
            table_one[i, :, k * LANES:(k + 1) * LANES] = (pair * col).astype(BF16)
            if k % 2 == 1:
                both = jnp.where(half_lane, jnp.broadcast_to(filters[:, k - 1:k], (channels, LANES)), col)
                at = basis * LANES + (k // 2) * LANES
                table_one[i, :, at:at + LANES] = (doubles[i + 2] * both).astype(BF16)

    replica_row = lax.broadcasted_iota(jnp.int32, (replicas, 1), 0)
    diagonal = (
        lax.broadcasted_iota(jnp.int32, (group, LANES), 0)
        == lax.broadcasted_iota(jnp.int32, (group, LANES), 1)
    )
    target = jnp.zeros((replicas, 1), F32)
    source = jnp.zeros((replicas, 1), jnp.int32)
    for r in range(replicas):
        target = jnp.where(replica_row == r, targets[r], target)
        source = jnp.where(replica_row == r, jnp.where(flags[r] > 0, slots[r], r), source)

    def spread_row(tile_list, e):
        tile = tile_list[e // 2]
        other = swap_halves(tile)
        first_half, second_half = (tile, other) if e % 2 == 0 else (other, tile)
        return [
            jnp.where(half_lane, first_half[2 * m:2 * m + 1], second_half[2 * m + 1:2 * m + 2])
            for m in range(tiles)
        ]

    def thirds(values):
        result = []
        for s in range(SPLITS):
            piece = values.astype(BF16).astype(F32)
            values = values - piece
            result.append(piece)
        return result

    middle = [0.5, 0.5, 0.5 * cells]
    eight_row = lax.broadcasted_iota(jnp.int32, (2 * group, lanes), 0)
    upper = eight_row < group
    own_lane = eight_row % group == lax.broadcasted_iota(jnp.int32, (2 * group, lanes), 1) // NA

    def gather_rows(values, odd):
        result = None
        for r in range(group):
            tile = values[:, (r // 2) * LANES:(r // 2 + 1) * LANES]
            if (r % 2 == 1) != odd:
                tile = swap_halves(tile)
            result = tile if result is None else jnp.where(member_row == r, tile, result)
        return jnp.broadcast_to(result, (group, LANES))

    def weigh(p, i, place_tiles):
        rows = []
        left_over = None
        for d in range(3):
            spread = jnp.concatenate(spread_row(place_tiles[d], i + 1), axis=1)
            mine[p, i, d] = jnp.broadcast_to(spread, (8, lanes))
            left_over = 1.0 - spread * spread if left_over is None else left_over - spread * spread
            rows.append(thirds(2.0 * spread))
        terms = [three[0] for three in rows for _ in range(SPLITS)]
        terms += [piece for three in rows for piece in (three[1], three[2], three[1])]
        terms += [jnp.full((1, lanes), -1.0, F32)] * SPLITS + thirds(left_over)
        for at in range(0, TERMS, 4):
            block = jnp.concatenate(
                [
                    jnp.where(own_lane, jnp.where(upper, terms[m], terms[m + 1]), 0.0)
                    for m in (at, at + 2)
                ],
                axis=0,
            )
            near_w[p, i, at * group:(at + 4) * group, :] = block.astype(BF16)

    def measure(p, i):
        window = cols[p, i * NA:i * NA + near, :]
        apart[p, i] = jnp.dot(window, near_w[p, i], preferred_element_type=F32)

    def pairs(p, i):
        mine_now = [jnp.concatenate([mine[p, i, d]] * (CHUNK // 8), axis=0) for d in range(3)]
        for at in range(0, near, CHUNK):
            row = i * NA + at
            inside = jnp.maximum(apart[p, i, at:at + CHUNK, :], 0.0)
            envelope = inside * inside
            for d in range(3):
                step = xb[p, d, row:row + CHUNK, :] - mine_now[d]
                vecs[p, i, d, at:at + CHUNK, :] = (step * envelope).astype(BF16)
            centered = 0.5 - inside
            power = (centered * (centered - 1.0 / (basis - 1))) * (-98.0 * LOG2E)
            start = (jnp.exp2(power) * envelope).astype(BF16)
            grow = jnp.exp2(centered * (28.0 * LOG2E)).astype(BF16)
            shrink = jnp.exp2(centered * (-28.0 * LOG2E)).astype(BF16)
            values = {basis // 2: start}
            for k in range(basis // 2, basis - 1):
                values[k + 1] = values[k] * grow
            for k in range(basis // 2, 0, -1):
                values[k - 1] = values[k] * shrink
            for k in range(basis):
                if at < 2 * NA:
                    to = k * LANES + at
                else:
                    to = basis * LANES + k * NA + at - 2 * NA
                gauss[p, i, to:to + CHUNK, :] = values[k]

    def gather_scalar(p, i):
        scalar = jnp.dot(table_one[i], gauss[p, i], preferred_element_type=F32)
        mixed[p, i, 0:channels, :] = scalar.astype(BF16)

    def gather_vector(p, i):
        norm = None
        for d in range(3):
            vec = jnp.dot(table_vec[i], vecs[p, i, d], preferred_element_type=F32)
            norm = vec * vec if norm is None else norm + vec * vec
        norm = norm * jnp.concatenate([scale_sq[...]] * tiles, axis=1)
        mixed[p, i, channels:, :] = norm.astype(BF16)

    def revise(p, i):
        half = jnp.dot(mix[...], mixed[p, i], preferred_element_type=F32)
        hidden = half * jnp.tanh(half) + half + jnp.concatenate([feat_t[i]] * tiles, axis=1)
        return hidden.astype(BF16)

    def project(hidden):
        return jnp.dot(later_t[...], hidden, preferred_element_type=F32).astype(BF16)

    def read(p, i, second):
        out = jnp.dot(read_two[...], second, preferred_element_type=F32)
        flats[p, i] = jnp.broadcast_to(out[0:1] + out[1:2], (8, lanes))

    def force(p, i):
        even, odd, last = [
            gather_rows(flats[p, i + j, 0:1, :], odd) for j, odd in ((-1, False), (0, True), (1, False))
        ]
        window = jnp.concatenate([jnp.where(half_lane, even, odd), jnp.where(half_lane, last, 0.0)], axis=1)
        window = window + s_one[:, i * NA:(i + 4) * NA]
        high, low = split_bf16(window)
        stacked = jnp.concatenate([high.astype(F32), low.astype(F32)], axis=0)
        stacked = jnp.concatenate([stacked] * (16 // (2 * group)), axis=0).astype(BF16)
        for d in range(3):
            out = jnp.dot(stacked, vecs[p, i, d], preferred_element_type=F32)
            pushes[p, i, d] = gather_rows(out[:group] + out[group:2 * group], i % 2 == 0)

    def is_moving(t):
        return jnp.where(t > 0, 1.0, 0.0).astype(F32)

    def vg_copies(t, p):
        return [
            remote(vg_send.at[t, p, 0], vg_recv.at[t, p, 1], vg_send_sem.at[t, p, 0], vg_recv_sem.at[t, p, 0], left),
            remote(vg_send.at[t, p, 1], vg_recv.at[t, p, 0], vg_send_sem.at[t, p, 1], vg_recv_sem.at[t, p, 1], right),
        ]

    def advance(t, p):
        moving = is_moving(t)
        pieces = []
        square = None
        place_tiles = []
        for d in range(3):
            half = state_v[p, d] + (0.5 * step_time) * state_g[p, d]
            x = state_x[p, d] + (moving * step_time) * half
            state_v[p, d] = half
            state_x[p, d] = x
            x = x - middle[d]
            place_tiles.append([x[:, at:at + LANES] for at in range(0, wide, LANES)])
            square = x * x if square is None else square + x * x
            pieces.append(thirds(x))
        stack = [piece for three in pieces for piece in three]
        stack += [piece for three in pieces for piece in (three[0], three[0], three[1])]
        stack += thirds(square)
        stack += [jnp.ones((SPLITS * group, wide), F32), jnp.zeros((LANES - TERMS * group, wide), F32)]
        tall = jnp.concatenate(stack, axis=0)
        for at in range(0, wide, LANES):
            cols[p, at:at + LANES, :] = tall[:, at:at + LANES].T.astype(BF16)
        for d in range(3):
            xb[p, d] = jnp.dot(cols[p, 0:ext * NA, :], selector[d], preferred_element_type=F32)
        def stage(i):
            if i + 1 < inner:
                weigh(p, i + 1, place_tiles)
            hidden = revise(p, i - 2) if i >= 2 else None
            if 1 <= i <= inner:
                gather_scalar(p, i - 1)
            if i + 1 < inner:
                measure(p, i + 1)
            second = project(hidden) if i >= 2 else None
            if 1 <= i <= inner:
                gather_vector(p, i - 1)
            if i >= 2:
                read(p, i - 2, second)
            if i < inner:
                pairs(p, i)

        weigh(p, 0, place_tiles)
        measure(p, 0)
        stage(0)
        for i in range(1, inner):
            pl.when(lax.rem((me + i) * (me + i + 1), 2) < 1)(functools.partial(stage, i))
        stage(inner)
        for i in range(1, inner - 3):
            force(p, i)
        hidden = revise(p, inner - 1)
        if inner > 3:
            force(p, inner - 3)
        read(p, inner - 1, project(hidden))
        force(p, inner - 2)
        kinetic = jnp.zeros((group, 1), F32)
        for d in range(3):
            joined = []
            for c in range(0, cells, 2):
                even = pushes[p, c + 1, d]
                odd = pushes[p, c + 2, d] if c + 1 < cells else jnp.zeros((group, LANES), F32)
                joined.append(jnp.where(half_lane, even, odd))
            g = jnp.concatenate(joined, axis=1)[:, :own]
            v = state_v[p, d, :, edge:edge + own] + (moving * (0.5 * step_time)) * g
            vg_send[t, p, 0, d] = jnp.concatenate([v[:, :edge], g[:, :edge]], axis=1)
            vg_send[t, p, 1, d] = jnp.concatenate([v[:, own - edge:], g[:, own - edge:]], axis=1)
            kinetic = kinetic + jnp.sum(v * v, axis=1, keepdims=True)
            state_v[p, d, :, edge:edge + own] = v
            state_g[p, d, :, edge:edge + own] = g
        across = jnp.sum(jnp.where(diagonal, kinetic, 0.0), axis=0, keepdims=True)
        kin_send[t, p] = across
        kin_recv[t, p, n - 1] = across

        def spread(d, inner_carry):
            remote(
                kin_send.at[t, p], kin_recv.at[t, p, d - 1], kin_send_sem.at[t, p],
                kin_recv_sem.at[t, p], lax.rem(me + d, n),
            ).start()
            return inner_carry

        for copy in vg_copies(t, p):
            copy.start()
        lax.fori_loop(1, n, spread, 0)

    def finish(t, p):
        everything = kin_recv.at[t, p, pl.ds(0, n - 1)]
        for copy in vg_copies(t, p):
            copy.wait()
        pltpu.make_async_copy(everything, everything, kin_send_sem.at[t, p]).wait()
        pltpu.make_async_copy(everything, everything, kin_recv_sem.at[t, p]).wait()
        collected = jnp.sum(kin_recv[t, p], axis=0)
        gathered = jnp.sum(jnp.where(diagonal, collected, 0.0), axis=1, keepdims=True)
        goal = target[p * group:(p + 1) * group]
        stretch = jnp.sqrt(goal / (gathered / (3.0 * own * n) + motion_work_lower_limit))
        stretch = jnp.where(t > 0, stretch, 1.0)
        rest = jnp.zeros((group, wide - ext * NA), F32)
        for d in range(3):
            from_left, from_right = vg_recv[t, p, 0, d], vg_recv[t, p, 1, d]
            state_v[p, d] = stretch * jnp.concatenate(
                [from_left[:, :edge], state_v[p, d, :, edge:edge + own], from_right[:, :edge], rest], axis=1
            )
            state_g[p, d, :, 0:edge] = from_left[:, edge:]
            state_g[p, d, :, edge + own:2 * edge + own] = from_right[:, edge:]

    def step(t, carry):
        for p in range(parts):
            pl.when(t > 0)(functools.partial(finish, t - 1, p))
            advance(t, p)
        return carry

    lax.fori_loop(0, STEPS + 1, step, 0)
    for p in range(parts):
        finish(STEPS, p)

    def pick(values):
        result = jnp.zeros_like(values)
        for r in range(replicas):
            result = jnp.where(source == r, values[r:r + 1], result)
        return result

    def whole(state, d):
        return jnp.concatenate([state[p, d, :, edge:edge + own] for p in range(parts)], axis=0)

    heat = jnp.sqrt(target / pick(target))
    floor = (lax.broadcasted_iota(jnp.int32, (1, own), 1) // NA).astype(F32)
    for d in range(3):
        x = pick(whole(state_x, d))
        if d == 2:
            x = x - floor
        places_out[d] = x
        speeds_out[d] = pick(whole(state_v, d)) * heat
        forces_out[d] = pick(whole(state_g, d))


def on_device(
    particle_places,
    particle_speeds,
    thermal_targets,
    element_features,
    swap_counterpart_slot,
    swap_approval_flags,
    initial_signal_projector,
    initial_distance_filter,
    initial_directional_scales,
    invariant_revision_matrix,
    magnitude_revision_matrix,
    later_signal_projector,
    later_directional_scales,
    push_output_matrix,
):
    n = lax.axis_size("dom")
    replicas, _, own = particle_places.shape
    cells = own // NA
    channels = element_features.shape[1]
    ext = cells + 2 * HALO
    inner = cells + 2
    edge = HALO * NA
    wide = -(-ext * NA // LANES) * LANES
    rounds = STEPS + 1
    group = 4
    parts = replicas // group
    lanes = group * NA
    basis = initial_distance_filter.shape[0]
    depth = basis * 3 * NA
    vmem = pl.BlockSpec(memory_space=pltpu.VMEM)
    smem = pl.BlockSpec(memory_space=pltpu.SMEM)
    outside = pl.BlockSpec(memory_space=pl.ANY)
    out = jax.ShapeDtypeStruct((3, replicas, own), F32)
    results = pl.pallas_call(
        functools.partial(kernel, n, replicas, cells, parts),
        out_shape=(out, out, out),
        in_specs=[outside, outside, smem, smem, smem] + [outside] * 9,
        out_specs=(vmem, vmem, vmem),
        scratch_shapes=[
            pltpu.VMEM((3, replicas, own), F32),
            pltpu.VMEM((3, replicas, own), F32),
            pltpu.VMEM((wide, channels), BF16),
            pltpu.VMEM((channels, channels), BF16),
            pltpu.VMEM((basis, channels), F32),
            pltpu.VMEM((1, channels), F32),
            pltpu.VMEM((channels, channels), BF16),
            pltpu.VMEM((channels, channels), BF16),
            pltpu.VMEM((channels, channels), BF16),
            pltpu.VMEM((1, channels), F32),
            pltpu.VMEM((1, channels), F32),
            pltpu.VMEM((2, 3, replicas, own), F32),
            pltpu.VMEM((inner, channels, depth), BF16),
            pltpu.VMEM((inner, channels, 4 * NA), BF16),
            pltpu.VMEM((inner, channels, LANES), F32),
            pltpu.VMEM((channels, 2 * channels), BF16),
            pltpu.VMEM((channels, channels), BF16),
            pltpu.VMEM((channels, LANES), F32),
            pltpu.VMEM((16, channels), BF16),
            pltpu.VMEM((1, wide + LANES), F32),
            pltpu.VMEM((3, LANES, lanes), BF16),
            pltpu.VMEM((parts, 3, group, wide), F32),
            pltpu.VMEM((parts, 3, group, wide), F32),
            pltpu.VMEM((parts, 3, group, wide), F32),
            pltpu.VMEM((parts, wide, LANES), BF16),
            pltpu.VMEM((parts, 3, ext * NA, lanes), F32),
            pltpu.VMEM((parts, inner, 3, 8, lanes), F32),
            pltpu.VMEM((parts, inner, LANES, lanes), BF16),
            pltpu.VMEM((parts, inner, 3 * NA, lanes), F32),
            pltpu.VMEM((parts, inner, depth, lanes), BF16),
            pltpu.VMEM((parts, inner, 3, 4 * NA, lanes), BF16),
            pltpu.VMEM((parts, inner, 2 * channels, lanes), BF16),
            pltpu.VMEM((parts, inner, 8, lanes), F32),
            pltpu.VMEM((parts, inner, 3, group, LANES), F32),
            pltpu.VMEM((rounds, parts, 2, 3, group, 2 * edge), F32),
            pltpu.VMEM((rounds, parts, 2, 3, group, 2 * edge), F32),
            pltpu.VMEM((rounds, parts, 1, LANES), F32),
            pltpu.VMEM((rounds, parts, n, 1, LANES), F32),
            pltpu.SemaphoreType.DMA((11,)),
            pltpu.SemaphoreType.DMA((4,)),
            pltpu.SemaphoreType.DMA((4,)),
            pltpu.SemaphoreType.DMA((rounds, parts, 2)),
            pltpu.SemaphoreType.DMA((rounds, parts, 2)),
            pltpu.SemaphoreType.DMA((rounds, parts)),
            pltpu.SemaphoreType.DMA((rounds, parts)),
        ],
        compiler_params=pltpu.CompilerParams(
            collective_id=0, has_side_effects=True, vmem_limit_bytes=63 * 1024 * 1024
        ),
    )(
        jnp.transpose(particle_places, (1, 0, 2)),
        jnp.transpose(particle_speeds, (1, 0, 2)),
        thermal_targets,
        swap_counterpart_slot,
        swap_approval_flags,
        element_features,
        initial_signal_projector,
        initial_distance_filter,
        initial_directional_scales.reshape(1, -1),
        invariant_revision_matrix,
        magnitude_revision_matrix,
        later_signal_projector,
        later_directional_scales.reshape(1, -1),
        push_output_matrix.reshape(1, -1),
    )
    return tuple(jnp.transpose(result, (1, 0, 2)) for result in results)
def solution(mesh):
    along = P("groups", None, "dom")
    return jax.shard_map(
        on_device,
        mesh=mesh,
        in_specs=(
            along,
            along,
            P("groups"),
            P(("groups", "dom"), None),
            P("groups"),
            P("groups"),
            P(),
            P(),
            P(),
            P(),
            P(),
            P(),
            P(),
            P(),
        ),
        out_specs=(along, along, along),
        check_vma=False,
    )
```

```python
import functools
import math

import jax
import jax.numpy as jnp
from jax import lax
from jax.experimental import pallas as pl
from jax.experimental.pallas import tpu as pltpu
from jax.sharding import PartitionSpec as P

NA = 64
STEPS = 4
LANES = 128
CHUNK = 16
HALO = 2
SPLITS = 3
TERMS = 24
LOG2E = math.log2(math.e)

step_time = 0.05
motion_work_lower_limit = 1e-06

F32 = jnp.float32
BF16 = jnp.bfloat16
MESH = pl.DeviceIdType.MESH


def split_bf16(values):
    high = values.astype(BF16)
    low = (values - high.astype(F32)).astype(BF16)
    return high, low


def weight_rows(weights):
    high, low = split_bf16(weights)
    high, low = high.astype(F32), low.astype(F32)
    row = lax.broadcasted_iota(jnp.int32, (16, weights.shape[1]), 0)
    return jnp.where(row == 0, high, jnp.where(row == 1, low, 0.0)).astype(BF16)


def swap_halves(values):
    return pltpu.roll(values, NA, 1)


def kernel(
    n, replicas, cells, parts,
    places, speeds, targets, slots, flags, features,
    projector, radial_filter, scales_one, invariant, magnitude, later_projector, scales_two, push,
    places_out, speeds_out, forces_out,
    own_places, own_speeds, feats, w_project, w_filter, w_scale_one, w_invariant, w_magnitude,
    w_later, w_scale_two, w_push,
    place_halo, table_one, table_vec, feat_t, mix, scale_sq, read_two, s_one, selector,
    state_x, state_v, state_g, cols, xb, mine, near_w, apart, gauss, vecs, mixed, flats, pushes,
    vg_send, vg_recv, kin_send, kin_recv,
    load_sem, init_send_sem, init_recv_sem, vg_send_sem, vg_recv_sem, kin_send_sem, kin_recv_sem,
):
    me = lax.axis_index("dom")
    left = lax.rem(me + n - 1, n)
    right = lax.rem(me + 1, n)
    own = cells * NA
    edge = HALO * NA
    ext = cells + 2 * HALO
    inner = cells + 2
    wide = state_x.shape[3]
    group = replicas // parts
    lanes = group * NA
    tiles = lanes // LANES
    channels = features.shape[1]
    basis = radial_filter.shape[0]
    near = 3 * NA

    barrier = pltpu.get_barrier_semaphore()

    def greet(d, carry):
        pl.semaphore_signal(barrier, inc=1, device_id={"dom": lax.rem(me + d, n)}, device_id_type=MESH)
        return carry

    loads = [
        (features, feats.at[pl.ds(edge, own)]),
        (projector, w_project),
        (places, own_places),
        (speeds, own_speeds),
        (radial_filter, w_filter),
        (scales_one, w_scale_one),
        (invariant, w_invariant),
        (magnitude, w_magnitude),
        (later_projector, w_later),
        (scales_two, w_scale_two),
        (push, w_push),
    ]
    loads = [pltpu.make_async_copy(src, dst, load_sem.at[i]) for i, (src, dst) in enumerate(loads)]
    for load in loads:
        load.start()
    lax.fori_loop(1, n, greet, 0)

    def remote(src, dst, send_sem, recv_sem, to):
        return pltpu.make_async_remote_copy(
            src_ref=src, dst_ref=dst, send_sem=send_sem, recv_sem=recv_sem,
            device_id={"dom": to}, device_id_type=MESH,
        )

    first = [
        remote(places, place_halo.at[1], init_send_sem.at[0], init_recv_sem.at[0], left),
        remote(places, place_halo.at[0], init_send_sem.at[1], init_recv_sem.at[1], right),
        remote(
            features.at[pl.ds(0, edge)], feats.at[pl.ds(edge + own, edge)],
            init_send_sem.at[2], init_recv_sem.at[2], left,
        ),
        remote(
            features.at[pl.ds(own - edge, edge)], feats.at[pl.ds(0, edge)],
            init_send_sem.at[3], init_recv_sem.at[3], right,
        ),
    ]
    pl.semaphore_wait(barrier, n - 1)
    for copy in first:
        copy.start()
    for load in loads:
        load.wait()

    half_lane = lax.broadcasted_iota(jnp.int32, (1, LANES), 1) < NA
    member_row = lax.broadcasted_iota(jnp.int32, (group, 1), 0)

    def flip(values):
        return values.astype(F32).T

    def column(row):
        return jnp.broadcast_to(row.T[:, 0:1], (channels, LANES))

    offset = lax.broadcasted_iota(jnp.int32, (basis, channels), 0).astype(F32) - 0.5 * (basis - 1)
    filters = (w_filter[...] * jnp.exp(-2.0 * offset * offset)).T
    push_row = w_push[...]
    w_one = weight_rows(w_scale_one[...] * push_row)
    back = lax.dot_general(
        weight_rows(w_scale_two[...] * push_row), w_later[...], (((1,), (1,)), ((), ())),
        preferred_element_type=F32,
    )
    read_two[...] = weight_rows(back[0:1] + back[1:2])
    scale_row = jnp.broadcast_to(w_scale_one[...] * w_scale_one[...], (8, channels))
    scale_sq[...] = column(scale_row)
    mix[:, 0:channels] = (0.5 * flip(w_invariant[...])).astype(BF16)
    mix[:, channels:2 * channels] = (0.5 * flip(w_magnitude[...])).astype(BF16)

    k_row = lax.broadcasted_iota(jnp.int32, (LANES, lanes), 0)
    k_lane = lax.broadcasted_iota(jnp.int32, (LANES, lanes), 1)
    for d in range(3):
        base = d * SPLITS * group
        inside = (k_row >= base) & (k_row < base + SPLITS * group)
        chosen = inside & ((k_row - base) % group == k_lane // NA)
        selector[d] = jnp.where(chosen, 1.0, 0.0).astype(BF16)
    for p in range(parts):
        for i in range(inner):
            for d in range(3):
                vecs[p, i, d, near:, :] = jnp.zeros((4 * NA - near, lanes), BF16)
            near_w[p, i, TERMS * group:, :] = jnp.zeros((LANES - TERMS * group, lanes), BF16)
    feats[ext * NA:, :] = jnp.zeros((wide - ext * NA, channels), BF16)

    total = cells * n
    floor_own = (me * cells).astype(F32)
    floor_left = (me * cells + jnp.where(me == 0, total, 0)).astype(F32)
    floor_right = (me * cells - jnp.where(me == n - 1, total, 0)).astype(F32)
    lift = [0.0, 0.0, 1.0]
    tail = jnp.zeros((group, wide - ext * NA), F32)
    for p in range(parts):
        members = slice(p * group, (p + 1) * group)
        for d in range(3):
            state_v[p, d] = jnp.concatenate(
                [jnp.zeros((group, edge), F32), own_speeds[d, members, :], jnp.zeros((group, edge), F32), tail],
                axis=1,
            )
            state_g[p, d] = jnp.zeros((group, wide), F32)

    for copy in first:
        copy.wait()

    for p in range(parts):
        members = slice(p * group, (p + 1) * group)
        for d in range(3):
            state_x[p, d] = jnp.concatenate(
                [
                    place_halo[0, d, members, own - edge:] - lift[d] * floor_left,
                    own_places[d, members, :] - lift[d] * floor_own,
                    place_halo[1, d, members, :edge] - lift[d] * floor_right,
                    tail,
                ],
                axis=1,
            )

    signals = jnp.dot(feats[...], w_project[...], preferred_element_type=F32).astype(BF16)
    signal_tiles = [flip(signals[at:at + LANES]) for at in range(0, wide, LANES)]
    feat_tiles = [flip(feats[at:at + LANES, :]) for at in range(0, wide, LANES)]

    def double(tile_list, e):
        tile = tile_list[e // 2]
        other = swap_halves(tile)
        return jnp.where(half_lane, tile, other) if e % 2 == 0 else jnp.where(half_lane, other, tile)

    doubles = [double(signal_tiles, e) for e in range(ext)]
    flat_signals = jnp.concatenate(signal_tiles, axis=1).astype(BF16)
    out = jnp.dot(w_one, flat_signals, preferred_element_type=F32)
    s_one[:, 0:wide] = out[0:1] + out[1:2]
    s_one[:, wide:] = jnp.zeros((1, LANES), F32)
    for i in range(inner):
        feat_t[i] = double(feat_tiles, i + 1)
        pair = jnp.where(half_lane, doubles[i], doubles[i + 1])
        table_vec[i, :, 0:LANES] = pair.astype(BF16)
        table_vec[i, :, LANES:2 * LANES] = jnp.where(half_lane, doubles[i + 2], 0.0).astype(BF16)
        for k in range(basis):
            col = jnp.broadcast_to(filters[:, k:k + 1], (channels, LANES))
            table_one[i, :, k * LANES:(k + 1) * LANES] = (pair * col).astype(BF16)
            if k % 2 == 1:
                both = jnp.where(half_lane, jnp.broadcast_to(filters[:, k - 1:k], (channels, LANES)), col)
                at = basis * LANES + (k // 2) * LANES
                table_one[i, :, at:at + LANES] = (doubles[i + 2] * both).astype(BF16)

    replica_row = lax.broadcasted_iota(jnp.int32, (replicas, 1), 0)
    diagonal = (
        lax.broadcasted_iota(jnp.int32, (group, LANES), 0)
        == lax.broadcasted_iota(jnp.int32, (group, LANES), 1)
    )
    target = jnp.zeros((replicas, 1), F32)
    source = jnp.zeros((replicas, 1), jnp.int32)
    for r in range(replicas):
        target = jnp.where(replica_row == r, targets[r], target)
        source = jnp.where(replica_row == r, jnp.where(flags[r] > 0, slots[r], r), source)

    def spread_row(tile_list, e):
        tile = tile_list[e // 2]
        other = swap_halves(tile)
        first_half, second_half = (tile, other) if e % 2 == 0 else (other, tile)
        return [
            jnp.where(half_lane, first_half[2 * m:2 * m + 1], second_half[2 * m + 1:2 * m + 2])
            for m in range(tiles)
        ]

    def thirds(values):
        result = []
        for s in range(SPLITS):
            piece = values.astype(BF16).astype(F32)
            values = values - piece
            result.append(piece)
        return result

    middle = [0.5, 0.5, 0.5 * cells]
    eight_row = lax.broadcasted_iota(jnp.int32, (2 * group, lanes), 0)
    upper = eight_row < group
    own_lane = eight_row % group == lax.broadcasted_iota(jnp.int32, (2 * group, lanes), 1) // NA

    def gather_rows(values, odd):
        result = None
        for r in range(group):
            tile = values[:, (r // 2) * LANES:(r // 2 + 1) * LANES]
            if (r % 2 == 1) != odd:
                tile = swap_halves(tile)
            result = tile if result is None else jnp.where(member_row == r, tile, result)
        return jnp.broadcast_to(result, (group, LANES))

    def weigh(p, i, place_tiles):
        rows = []
        left_over = None
        for d in range(3):
            spread = jnp.concatenate(spread_row(place_tiles[d], i + 1), axis=1)
            mine[p, i, d] = jnp.broadcast_to(spread, (8, lanes))
            left_over = 1.0 - spread * spread if left_over is None else left_over - spread * spread
            rows.append(thirds(2.0 * spread))
        terms = [three[0] for three in rows for _ in range(SPLITS)]
        terms += [piece for three in rows for piece in (three[1], three[2], three[1])]
        terms += [jnp.full((1, lanes), -1.0, F32)] * SPLITS + thirds(left_over)
        for at in range(0, TERMS, 4):
            block = jnp.concatenate(
                [
                    jnp.where(own_lane, jnp.where(upper, terms[m], terms[m + 1]), 0.0)
                    for m in (at, at + 2)
                ],
                axis=0,
            )
            near_w[p, i, at * group:(at + 4) * group, :] = block.astype(BF16)

    def measure(p, i):
        window = cols[p, i * NA:i * NA + near, :]
        apart[p, i] = jnp.dot(window, near_w[p, i], preferred_element_type=F32)

    def pairs(p, i, begin, end):
        mine_now = [jnp.concatenate([mine[p, i, d]] * (CHUNK // 8), axis=0) for d in range(3)]
        for at in range(begin * CHUNK, end * CHUNK, CHUNK):
            row = i * NA + at
            inside = jnp.maximum(apart[p, i, at:at + CHUNK, :], 0.0)
            envelope = inside * inside
            for d in range(3):
                step = xb[p, d, row:row + CHUNK, :] - mine_now[d]
                vecs[p, i, d, at:at + CHUNK, :] = (step * envelope).astype(BF16)
            centered = 0.5 - inside
            power = (centered * (centered - 1.0 / (basis - 1))) * (-98.0 * LOG2E)
            start = (jnp.exp2(power) * envelope).astype(BF16)
            grow = jnp.exp2(centered * (28.0 * LOG2E)).astype(BF16)
            shrink = jnp.exp2(centered * (-28.0 * LOG2E)).astype(BF16)
            values = {basis // 2: start}
            for k in range(basis // 2, basis - 1):
                values[k + 1] = values[k] * grow
            for k in range(basis // 2, 0, -1):
                values[k - 1] = values[k] * shrink
            for k in range(basis):
                if at < 2 * NA:
                    to = k * LANES + at
                else:
                    to = basis * LANES + k * NA + at - 2 * NA
                gauss[p, i, to:to + CHUNK, :] = values[k]

    def gather_scalar(p, i, between):
        depth = table_one.shape[2] // len(between)
        scalar = None
        for m, fill in enumerate(between):
            part = slice(m * depth, (m + 1) * depth)
            term = jnp.dot(table_one[i, :, part], gauss[p, i, part, :], preferred_element_type=F32)
            scalar = term if scalar is None else scalar + term
            fill()
        mixed[p, i, 0:channels, :] = scalar.astype(BF16)

    def gather_vector(p, i, between):
        norm = None
        for d in range(3):
            vec = jnp.dot(table_vec[i], vecs[p, i, d], preferred_element_type=F32)
            norm = vec * vec if norm is None else norm + vec * vec
            between[d]()
        norm = norm * jnp.concatenate([scale_sq[...]] * tiles, axis=1)
        mixed[p, i, channels:, :] = norm.astype(BF16)

    def revise(p, i):
        half = jnp.dot(mix[...], mixed[p, i], preferred_element_type=F32)
        hidden = half * jnp.tanh(half) + half + jnp.concatenate([feat_t[i]] * tiles, axis=1)
        return hidden.astype(BF16)

    def read(p, i, hidden):
        out = jnp.dot(read_two[...], hidden, preferred_element_type=F32)
        flats[p, i] = jnp.broadcast_to(out[0:1] + out[1:2], (8, lanes))

    def force(p, i):
        even, odd, last = [
            gather_rows(flats[p, i + j, 0:1, :], odd) for j, odd in ((-1, False), (0, True), (1, False))
        ]
        window = jnp.concatenate([jnp.where(half_lane, even, odd), jnp.where(half_lane, last, 0.0)], axis=1)
        window = window + s_one[:, i * NA:(i + 4) * NA]
        high, low = split_bf16(window)
        stacked = jnp.concatenate([high.astype(F32), low.astype(F32)], axis=0)
        stacked = jnp.concatenate([stacked] * (16 // (2 * group)), axis=0).astype(BF16)
        for d in range(3):
            out = jnp.dot(stacked, vecs[p, i, d], preferred_element_type=F32)
            pushes[p, i, d] = gather_rows(out[:group] + out[group:2 * group], i % 2 == 0)

    def is_moving(t):
        return jnp.where(t > 0, 1.0, 0.0).astype(F32)

    def vg_copies(t, p):
        return [
            remote(vg_send.at[t, p, 0], vg_recv.at[t, p, 1], vg_send_sem.at[t, p, 0], vg_recv_sem.at[t, p, 0], left),
            remote(vg_send.at[t, p, 1], vg_recv.at[t, p, 0], vg_send_sem.at[t, p, 1], vg_recv_sem.at[t, p, 1], right),
        ]

    def advance(t, p):
        moving = is_moving(t)
        pieces = []
        square = None
        place_tiles = []
        for d in range(3):
            half = state_v[p, d] + (0.5 * step_time) * state_g[p, d]
            x = state_x[p, d] + (moving * step_time) * half
            state_v[p, d] = half
            state_x[p, d] = x
            x = x - middle[d]
            place_tiles.append([x[:, at:at + LANES] for at in range(0, wide, LANES)])
            square = x * x if square is None else square + x * x
            pieces.append(thirds(x))
        stack = [piece for three in pieces for piece in three]
        stack += [piece for three in pieces for piece in (three[0], three[0], three[1])]
        stack += thirds(square)
        stack += [jnp.ones((SPLITS * group, wide), F32), jnp.zeros((LANES - TERMS * group, wide), F32)]
        tall = jnp.concatenate(stack, axis=0)
        for at in range(0, wide, LANES):
            cols[p, at:at + LANES, :] = tall[:, at:at + LANES].T.astype(BF16)
        for d in range(3):
            xb[p, d] = jnp.dot(cols[p, 0:ext * NA, :], selector[d], preferred_element_type=F32)
        def stage(i):
            count = near // CHUNK

            def some(begin, end):
                if i < inner:
                    pairs(p, i, count * begin // 12, count * end // 12)

            hidden = revise(p, i - 2) if i >= 2 else None
            some(0, 1)
            if 1 <= i <= inner:
                gather_scalar(p, i - 1, [functools.partial(some, *span) for span in ((1, 2), (2, 3), (3, 4), (4, 5), (5, 6), (6, 6))])
            else:
                some(1, 6)
            if i + 1 < inner:
                weigh(p, i + 1, place_tiles)
                measure(p, i + 1)
            some(6, 7)
            if i >= 2:
                read(p, i - 2, hidden)
            some(7, 8)
            if 1 <= i <= inner:
                gather_vector(p, i - 1, [functools.partial(some, *span) for span in ((8, 9), (9, 10), (10, 11))])
            else:
                some(8, 11)
            some(11, 12)

        weigh(p, 0, place_tiles)
        measure(p, 0)
        stage(0)
        for i in range(1, inner):
            pl.when(lax.rem((me + i) * (me + i + 1), 2) < 1)(functools.partial(stage, i))
        empty = [lambda: None] * 3
        gather_scalar(p, inner - 1, empty[:1])
        hidden = revise(p, inner - 2)
        gather_vector(p, inner - 1, empty)
        read(p, inner - 2, hidden)
        for i in range(1, inner - 3):
            force(p, i)
        hidden = revise(p, inner - 1)
        for i in range(max(1, inner - 3), inner - 2):
            force(p, i)
        read(p, inner - 1, hidden)
        force(p, inner - 2)
        kinetic = jnp.zeros((group, 1), F32)
        for d in range(3):
            joined = []
            for c in range(0, cells, 2):
                even = pushes[p, c + 1, d]
                odd = pushes[p, c + 2, d] if c + 1 < cells else jnp.zeros((group, LANES), F32)
                joined.append(jnp.where(half_lane, even, odd))
            g = jnp.concatenate(joined, axis=1)[:, :own]
            v = state_v[p, d, :, edge:edge + own] + (moving * (0.5 * step_time)) * g
            vg_send[t, p, 0, d] = jnp.concatenate([v[:, :edge], g[:, :edge]], axis=1)
            vg_send[t, p, 1, d] = jnp.concatenate([v[:, own - edge:], g[:, own - edge:]], axis=1)
            kinetic = kinetic + jnp.sum(v * v, axis=1, keepdims=True)
            state_v[p, d, :, edge:edge + own] = v
            state_g[p, d, :, edge:edge + own] = g
        across = jnp.sum(jnp.where(diagonal, kinetic, 0.0), axis=0, keepdims=True)
        kin_send[t, p] = across
        kin_recv[t, p, n - 1] = across

        def spread(d, inner_carry):
            remote(
                kin_send.at[t, p], kin_recv.at[t, p, d - 1], kin_send_sem.at[t, p],
                kin_recv_sem.at[t, p], lax.rem(me + d, n),
            ).start()
            return inner_carry

        for copy in vg_copies(t, p):
            copy.start()
        lax.fori_loop(1, n, spread, 0)

    def finish(t, p):
        everything = kin_recv.at[t, p, pl.ds(0, n - 1)]
        for copy in vg_copies(t, p):
            copy.wait()
        pltpu.make_async_copy(everything, everything, kin_send_sem.at[t, p]).wait()
        pltpu.make_async_copy(everything, everything, kin_recv_sem.at[t, p]).wait()
        collected = jnp.sum(kin_recv[t, p], axis=0)
        gathered = jnp.sum(jnp.where(diagonal, collected, 0.0), axis=1, keepdims=True)
        goal = target[p * group:(p + 1) * group]
        stretch = jnp.sqrt(goal / (gathered / (3.0 * own * n) + motion_work_lower_limit))
        stretch = jnp.where(t > 0, stretch, 1.0)
        rest = jnp.zeros((group, wide - ext * NA), F32)
        for d in range(3):
            from_left, from_right = vg_recv[t, p, 0, d], vg_recv[t, p, 1, d]
            state_v[p, d] = stretch * jnp.concatenate(
                [from_left[:, :edge], state_v[p, d, :, edge:edge + own], from_right[:, :edge], rest], axis=1
            )
            state_g[p, d, :, 0:edge] = from_left[:, edge:]
            state_g[p, d, :, edge + own:2 * edge + own] = from_right[:, edge:]

    def step(t, carry):
        for p in range(parts):
            pl.when(t > 0)(functools.partial(finish, t - 1, p))
            advance(t, p)
        return carry

    lax.fori_loop(0, STEPS + 1, step, 0)
    for p in range(parts):
        finish(STEPS, p)

    def pick(values):
        result = jnp.zeros_like(values)
        for r in range(replicas):
            result = jnp.where(source == r, values[r:r + 1], result)
        return result

    def whole(state, d):
        return jnp.concatenate([state[p, d, :, edge:edge + own] for p in range(parts)], axis=0)

    heat = jnp.sqrt(target / pick(target))
    floor = (lax.broadcasted_iota(jnp.int32, (1, own), 1) // NA).astype(F32)
    for d in range(3):
        x = pick(whole(state_x, d))
        if d == 2:
            x = x - floor
        places_out[d] = x
        speeds_out[d] = pick(whole(state_v, d)) * heat
        forces_out[d] = pick(whole(state_g, d))


def on_device(
    particle_places,
    particle_speeds,
    thermal_targets,
    element_features,
    swap_counterpart_slot,
    swap_approval_flags,
    initial_signal_projector,
    initial_distance_filter,
    initial_directional_scales,
    invariant_revision_matrix,
    magnitude_revision_matrix,
    later_signal_projector,
    later_directional_scales,
    push_output_matrix,
):
    n = lax.axis_size("dom")
    replicas, _, own = particle_places.shape
    cells = own // NA
    channels = element_features.shape[1]
    ext = cells + 2 * HALO
    inner = cells + 2
    edge = HALO * NA
    wide = -(-ext * NA // LANES) * LANES
    rounds = STEPS + 1
    group = 4
    parts = replicas // group
    lanes = group * NA
    basis = initial_distance_filter.shape[0]
    depth = basis * 3 * NA
    vmem = pl.BlockSpec(memory_space=pltpu.VMEM)
    smem = pl.BlockSpec(memory_space=pltpu.SMEM)
    outside = pl.BlockSpec(memory_space=pl.ANY)
    out = jax.ShapeDtypeStruct((3, replicas, own), F32)
    results = pl.pallas_call(
        functools.partial(kernel, n, replicas, cells, parts),
        out_shape=(out, out, out),
        in_specs=[outside, outside, smem, smem, smem] + [outside] * 9,
        out_specs=(vmem, vmem, vmem),
        scratch_shapes=[
            pltpu.VMEM((3, replicas, own), F32),
            pltpu.VMEM((3, replicas, own), F32),
            pltpu.VMEM((wide, channels), BF16),
            pltpu.VMEM((channels, channels), BF16),
            pltpu.VMEM((basis, channels), F32),
            pltpu.VMEM((1, channels), F32),
            pltpu.VMEM((channels, channels), BF16),
            pltpu.VMEM((channels, channels), BF16),
            pltpu.VMEM((channels, channels), BF16),
            pltpu.VMEM((1, channels), F32),
            pltpu.VMEM((1, channels), F32),
            pltpu.VMEM((2, 3, replicas, own), F32),
            pltpu.VMEM((inner, channels, depth), BF16),
            pltpu.VMEM((inner, channels, 4 * NA), BF16),
            pltpu.VMEM((inner, channels, LANES), F32),
            pltpu.VMEM((channels, 2 * channels), BF16),
            pltpu.VMEM((channels, LANES), F32),
            pltpu.VMEM((16, channels), BF16),
            pltpu.VMEM((1, wide + LANES), F32),
            pltpu.VMEM((3, LANES, lanes), BF16),
            pltpu.VMEM((parts, 3, group, wide), F32),
            pltpu.VMEM((parts, 3, group, wide), F32),
            pltpu.VMEM((parts, 3, group, wide), F32),
            pltpu.VMEM((parts, wide, LANES), BF16),
            pltpu.VMEM((parts, 3, ext * NA, lanes), F32),
            pltpu.VMEM((parts, inner, 3, 8, lanes), F32),
            pltpu.VMEM((parts, inner, LANES, lanes), BF16),
            pltpu.VMEM((parts, inner, 3 * NA, lanes), F32),
            pltpu.VMEM((parts, inner, depth, lanes), BF16),
            pltpu.VMEM((parts, inner, 3, 4 * NA, lanes), BF16),
            pltpu.VMEM((parts, inner, 2 * channels, lanes), BF16),
            pltpu.VMEM((parts, inner, 8, lanes), F32),
            pltpu.VMEM((parts, inner, 3, group, LANES), F32),
            pltpu.VMEM((rounds, parts, 2, 3, group, 2 * edge), F32),
            pltpu.VMEM((rounds, parts, 2, 3, group, 2 * edge), F32),
            pltpu.VMEM((rounds, parts, 1, LANES), F32),
            pltpu.VMEM((rounds, parts, n, 1, LANES), F32),
            pltpu.SemaphoreType.DMA((11,)),
            pltpu.SemaphoreType.DMA((4,)),
            pltpu.SemaphoreType.DMA((4,)),
            pltpu.SemaphoreType.DMA((rounds, parts, 2)),
            pltpu.SemaphoreType.DMA((rounds, parts, 2)),
            pltpu.SemaphoreType.DMA((rounds, parts)),
            pltpu.SemaphoreType.DMA((rounds, parts)),
        ],
        compiler_params=pltpu.CompilerParams(
            collective_id=0, has_side_effects=True, vmem_limit_bytes=63 * 1024 * 1024
        ),
    )(
        jnp.transpose(particle_places, (1, 0, 2)),
        jnp.transpose(particle_speeds, (1, 0, 2)),
        thermal_targets,
        swap_counterpart_slot,
        swap_approval_flags,
        element_features,
        initial_signal_projector,
        initial_distance_filter,
        initial_directional_scales.reshape(1, -1),
        invariant_revision_matrix,
        magnitude_revision_matrix,
        later_signal_projector,
        later_directional_scales.reshape(1, -1),
        push_output_matrix.reshape(1, -1),
    )
    return tuple(jnp.transpose(result, (1, 0, 2)) for result in results)
def solution(mesh):
    along = P("groups", None, "dom")
    return jax.shard_map(
        on_device,
        mesh=mesh,
        in_specs=(
            along,
            along,
            P("groups"),
            P(("groups", "dom"), None),
            P("groups"),
            P("groups"),
            P(),
            P(),
            P(),
            P(),
            P(),
            P(),
            P(),
            P(),
        ),
        out_specs=(along, along, along),
        check_vma=False,
    )
```

```python
import functools
import math

import jax
import jax.numpy as jnp
from jax import lax
from jax.experimental import pallas as pl
from jax.experimental.pallas import tpu as pltpu
from jax.sharding import PartitionSpec as P

NA = 64
STEPS = 4
LANES = 128
CHUNK = 16
HALO = 2
SPLITS = 3
TERMS = 24
LOG2E = math.log2(math.e)

step_time = 0.05
motion_work_lower_limit = 1e-06

F32 = jnp.float32
BF16 = jnp.bfloat16
MESH = pl.DeviceIdType.MESH


def split_bf16(values):
    high = values.astype(BF16)
    low = (values - high.astype(F32)).astype(BF16)
    return high, low


def weight_rows(weights):
    high, low = split_bf16(weights)
    high, low = high.astype(F32), low.astype(F32)
    row = lax.broadcasted_iota(jnp.int32, (16, weights.shape[1]), 0)
    return jnp.where(row == 0, high, jnp.where(row == 1, low, 0.0)).astype(BF16)


def swap_halves(values):
    return pltpu.roll(values, NA, 1)


def kernel(
    n, replicas, cells, parts,
    places, speeds, targets, slots, flags, features,
    projector, radial_filter, scales_one, invariant, magnitude, later_projector, scales_two, push,
    places_out, speeds_out, forces_out,
    own_places, own_speeds, feats, w_project, w_filter, w_scale_one, w_invariant, w_magnitude,
    w_later, w_scale_two, w_push,
    place_halo, table_one, table_vec, feat_t, mix, scale_sq, read_two, s_one, selector,
    state_x, state_v, state_g, cols, xb, mine, near_w, apart, gauss, vecs, mixed, flats, pushes,
    vg_send, vg_recv, kin_send, kin_recv,
    load_sem, init_send_sem, init_recv_sem, vg_send_sem, vg_recv_sem, kin_send_sem, kin_recv_sem,
):
    me = lax.axis_index("dom")
    left = lax.rem(me + n - 1, n)
    right = lax.rem(me + 1, n)
    own = cells * NA
    edge = HALO * NA
    ext = cells + 2 * HALO
    inner = cells + 2
    wide = state_x.shape[3]
    group = replicas // parts
    lanes = group * NA
    tiles = lanes // LANES
    channels = features.shape[1]
    basis = radial_filter.shape[0]
    near = 3 * NA

    barrier = pltpu.get_barrier_semaphore()

    def greet(d, carry):
        pl.semaphore_signal(barrier, inc=1, device_id={"dom": lax.rem(me + d, n)}, device_id_type=MESH)
        return carry

    loads = [
        (features, feats.at[pl.ds(edge, own)]),
        (projector, w_project),
        (places, own_places),
        (speeds, own_speeds),
        (radial_filter, w_filter),
        (scales_one, w_scale_one),
        (invariant, w_invariant),
        (magnitude, w_magnitude),
        (later_projector, w_later),
        (scales_two, w_scale_two),
        (push, w_push),
    ]
    loads = [pltpu.make_async_copy(src, dst, load_sem.at[i]) for i, (src, dst) in enumerate(loads)]
    for load in loads:
        load.start()
    lax.fori_loop(1, n, greet, 0)

    def remote(src, dst, send_sem, recv_sem, to):
        return pltpu.make_async_remote_copy(
            src_ref=src, dst_ref=dst, send_sem=send_sem, recv_sem=recv_sem,
            device_id={"dom": to}, device_id_type=MESH,
        )

    first = [
        remote(places, place_halo.at[1], init_send_sem.at[0], init_recv_sem.at[0], left),
        remote(places, place_halo.at[0], init_send_sem.at[1], init_recv_sem.at[1], right),
        remote(
            features.at[pl.ds(0, edge)], feats.at[pl.ds(edge + own, edge)],
            init_send_sem.at[2], init_recv_sem.at[2], left,
        ),
        remote(
            features.at[pl.ds(own - edge, edge)], feats.at[pl.ds(0, edge)],
            init_send_sem.at[3], init_recv_sem.at[3], right,
        ),
    ]
    pl.semaphore_wait(barrier, n - 1)
    for copy in first:
        copy.start()
    for load in loads:
        load.wait()

    half_lane = lax.broadcasted_iota(jnp.int32, (1, LANES), 1) < NA
    member_row = lax.broadcasted_iota(jnp.int32, (group, 1), 0)

    def flip(values):
        return values.astype(F32).T

    def column(row):
        return jnp.broadcast_to(row.T[:, 0:1], (channels, LANES))

    offset = lax.broadcasted_iota(jnp.int32, (basis, channels), 0).astype(F32) - 0.5 * (basis - 1)
    filters = (w_filter[...] * jnp.exp(-2.0 * offset * offset)).T
    push_row = w_push[...]
    w_one = weight_rows(w_scale_one[...] * push_row)
    back = lax.dot_general(
        weight_rows(w_scale_two[...] * push_row), w_later[...], (((1,), (1,)), ((), ())),
        preferred_element_type=F32,
    )
    read_two[...] = weight_rows(back[0:1] + back[1:2])
    scale_row = jnp.broadcast_to(w_scale_one[...] * w_scale_one[...], (8, channels))
    scale_sq[...] = column(scale_row)
    mix[:, 0:channels] = (0.5 * flip(w_invariant[...])).astype(BF16)
    mix[:, channels:2 * channels] = (0.5 * flip(w_magnitude[...])).astype(BF16)

    k_row = lax.broadcasted_iota(jnp.int32, (LANES, lanes), 0)
    k_lane = lax.broadcasted_iota(jnp.int32, (LANES, lanes), 1)
    for d in range(3):
        base = d * SPLITS * group
        inside = (k_row >= base) & (k_row < base + SPLITS * group)
        chosen = inside & ((k_row - base) % group == k_lane // NA)
        selector[d] = jnp.where(chosen, 1.0, 0.0).astype(BF16)
    for p in range(parts):
        for i in range(inner):
            for d in range(3):
                vecs[p, i, d, near:, :] = jnp.zeros((4 * NA - near, lanes), BF16)
            near_w[p, i, TERMS * group:, :] = jnp.zeros((LANES - TERMS * group, lanes), BF16)
    feats[ext * NA:, :] = jnp.zeros((wide - ext * NA, channels), BF16)

    total = cells * n
    floor_own = (me * cells).astype(F32)
    floor_left = (me * cells + jnp.where(me == 0, total, 0)).astype(F32)
    floor_right = (me * cells - jnp.where(me == n - 1, total, 0)).astype(F32)
    lift = [0.0, 0.0, 1.0]
    tail = jnp.zeros((group, wide - ext * NA), F32)
    for p in range(parts):
        members = slice(p * group, (p + 1) * group)
        for d in range(3):
            state_v[p, d] = jnp.concatenate(
                [jnp.zeros((group, edge), F32), own_speeds[d, members, :], jnp.zeros((group, edge), F32), tail],
                axis=1,
            )
            state_g[p, d] = jnp.zeros((group, wide), F32)

    for copy in first:
        copy.wait()

    for p in range(parts):
        members = slice(p * group, (p + 1) * group)
        for d in range(3):
            state_x[p, d] = jnp.concatenate(
                [
                    place_halo[0, d, members, own - edge:] - lift[d] * floor_left,
                    own_places[d, members, :] - lift[d] * floor_own,
                    place_halo[1, d, members, :edge] - lift[d] * floor_right,
                    tail,
                ],
                axis=1,
            )

    signals = jnp.dot(feats[...], w_project[...], preferred_element_type=F32).astype(BF16)
    signal_tiles = [flip(signals[at:at + LANES]) for at in range(0, wide, LANES)]
    feat_tiles = [flip(feats[at:at + LANES, :]) for at in range(0, wide, LANES)]

    def double(tile_list, e):
        tile = tile_list[e // 2]
        other = swap_halves(tile)
        return jnp.where(half_lane, tile, other) if e % 2 == 0 else jnp.where(half_lane, other, tile)

    doubles = [double(signal_tiles, e) for e in range(ext)]
    flat_signals = jnp.concatenate(signal_tiles, axis=1).astype(BF16)
    out = jnp.dot(w_one, flat_signals, preferred_element_type=F32)
    s_one[:, 0:wide] = out[0:1] + out[1:2]
    s_one[:, wide:] = jnp.zeros((1, LANES), F32)
    for i in range(inner):
        feat_t[i] = double(feat_tiles, i + 1)
        pair = jnp.where(half_lane, doubles[i], doubles[i + 1])
        table_vec[i, :, 0:LANES] = pair.astype(BF16)
        table_vec[i, :, LANES:2 * LANES] = jnp.where(half_lane, doubles[i + 2], 0.0).astype(BF16)
        for k in range(basis):
            col = jnp.broadcast_to(filters[:, k:k + 1], (channels, LANES))
            table_one[i, :, k * LANES:(k + 1) * LANES] = (pair * col).astype(BF16)
            if k % 2 == 1:
                both = jnp.where(half_lane, jnp.broadcast_to(filters[:, k - 1:k], (channels, LANES)), col)
                at = basis * LANES + (k // 2) * LANES
                table_one[i, :, at:at + LANES] = (doubles[i + 2] * both).astype(BF16)

    replica_row = lax.broadcasted_iota(jnp.int32, (replicas, 1), 0)
    diagonal = (
        lax.broadcasted_iota(jnp.int32, (group, LANES), 0)
        == lax.broadcasted_iota(jnp.int32, (group, LANES), 1)
    )
    target = jnp.zeros((replicas, 1), F32)
    source = jnp.zeros((replicas, 1), jnp.int32)
    for r in range(replicas):
        target = jnp.where(replica_row == r, targets[r], target)
        source = jnp.where(replica_row == r, jnp.where(flags[r] > 0, slots[r], r), source)

    def spread_row(tile_list, e):
        tile = tile_list[e // 2]
        other = swap_halves(tile)
        first_half, second_half = (tile, other) if e % 2 == 0 else (other, tile)
        return [
            jnp.where(half_lane, first_half[2 * m:2 * m + 1], second_half[2 * m + 1:2 * m + 2])
            for m in range(tiles)
        ]

    def thirds(values):
        result = []
        for s in range(SPLITS):
            piece = values.astype(BF16).astype(F32)
            values = values - piece
            result.append(piece)
        return result

    middle = [0.5, 0.5, 0.5 * cells]
    eight_row = lax.broadcasted_iota(jnp.int32, (2 * group, lanes), 0)
    upper = eight_row < group
    own_lane = eight_row % group == lax.broadcasted_iota(jnp.int32, (2 * group, lanes), 1) // NA

    def gather_rows(values, odd):
        result = None
        for r in range(group):
            tile = values[:, (r // 2) * LANES:(r // 2 + 1) * LANES]
            if (r % 2 == 1) != odd:
                tile = swap_halves(tile)
            result = tile if result is None else jnp.where(member_row == r, tile, result)
        return jnp.broadcast_to(result, (group, LANES))

    def weigh(p, i, place_tiles):
        rows = []
        left_over = None
        for d in range(3):
            spread = jnp.concatenate(spread_row(place_tiles[d], i + 1), axis=1)
            mine[p, i, d] = jnp.broadcast_to(spread, (8, lanes))
            left_over = 1.0 - spread * spread if left_over is None else left_over - spread * spread
            rows.append(thirds(2.0 * spread))
        terms = [three[0] for three in rows for _ in range(SPLITS)]
        terms += [piece for three in rows for piece in (three[1], three[2], three[1])]
        terms += [jnp.full((1, lanes), -1.0, F32)] * SPLITS + thirds(left_over)
        for at in range(0, TERMS, 4):
            block = jnp.concatenate(
                [
                    jnp.where(own_lane, jnp.where(upper, terms[m], terms[m + 1]), 0.0)
                    for m in (at, at + 2)
                ],
                axis=0,
            )
            near_w[p, i, at * group:(at + 4) * group, :] = block.astype(BF16)

    def measure(p, i):
        window = cols[p, i * NA:i * NA + near, :]
        apart[p, i] = jnp.dot(window, near_w[p, i], preferred_element_type=F32)

    def pairs(p, i, begin, end):
        mine_now = [jnp.concatenate([mine[p, i, d]] * (CHUNK // 8), axis=0) for d in range(3)]
        for at in range(begin * CHUNK, end * CHUNK, CHUNK):
            row = i * NA + at
            inside = jnp.maximum(apart[p, i, at:at + CHUNK, :], 0.0)
            envelope = inside * inside
            for d in range(3):
                step = xb[p, d, row:row + CHUNK, :] - mine_now[d]
                vecs[p, i, d, at:at + CHUNK, :] = (step * envelope).astype(BF16)
            centered = 0.5 - inside
            power = (centered * (centered - 1.0 / (basis - 1))) * (-98.0 * LOG2E)
            start = (jnp.exp2(power) * envelope).astype(BF16)
            grow = jnp.exp2(centered * (28.0 * LOG2E)).astype(BF16)
            shrink = jnp.exp2(centered * (-28.0 * LOG2E)).astype(BF16)
            values = {basis // 2: start}
            for k in range(basis // 2, basis - 1):
                values[k + 1] = values[k] * grow
            for k in range(basis // 2, 0, -1):
                values[k - 1] = values[k] * shrink
            for k in range(basis):
                if at < 2 * NA:
                    to = k * LANES + at
                else:
                    to = basis * LANES + k * NA + at - 2 * NA
                gauss[p, i, to:to + CHUNK, :] = values[k]

    def gather_scalar(p, i, between):
        depth = table_one.shape[2] // len(between)
        scalar = None
        for m, fill in enumerate(between):
            part = slice(m * depth, (m + 1) * depth)
            term = jnp.dot(table_one[i, :, part], gauss[p, i, part, :], preferred_element_type=F32)
            scalar = term if scalar is None else scalar + term
            fill()
        mixed[p, i, 0:channels, :] = scalar.astype(BF16)

    def gather_vector(p, i, between):
        norm = None
        for d in range(3):
            vec = jnp.dot(table_vec[i], vecs[p, i, d], preferred_element_type=F32)
            norm = vec * vec if norm is None else norm + vec * vec
            between[d]()
        norm = norm * jnp.concatenate([scale_sq[...]] * tiles, axis=1)
        mixed[p, i, channels:, :] = norm.astype(BF16)

    def revise(p, i):
        half = jnp.dot(mix[...], mixed[p, i], preferred_element_type=F32)
        hidden = half * jnp.tanh(half) + half + jnp.concatenate([feat_t[i]] * tiles, axis=1)
        return hidden.astype(BF16)

    def read(p, i, hidden):
        out = jnp.dot(read_two[...], hidden, preferred_element_type=F32)
        flats[p, i] = jnp.broadcast_to(out[0:1] + out[1:2], (8, lanes))

    def force(p, i):
        even, odd, last = [
            gather_rows(flats[p, i + j, 0:1, :], odd) for j, odd in ((-1, False), (0, True), (1, False))
        ]
        window = jnp.concatenate([jnp.where(half_lane, even, odd), jnp.where(half_lane, last, 0.0)], axis=1)
        window = window + s_one[:, i * NA:(i + 4) * NA]
        high, low = split_bf16(window)
        stacked = jnp.concatenate([high.astype(F32), low.astype(F32)], axis=0)
        stacked = jnp.concatenate([stacked] * (16 // (2 * group)), axis=0).astype(BF16)
        for d in range(3):
            out = jnp.dot(stacked, vecs[p, i, d], preferred_element_type=F32)
            pushes[p, i, d] = gather_rows(out[:group] + out[group:2 * group], i % 2 == 0)

    def is_moving(t):
        return jnp.where(t > 0, 1.0, 0.0).astype(F32)

    def vg_copies(t, p):
        return [
            remote(vg_send.at[t, p, 0], vg_recv.at[t, p, 1], vg_send_sem.at[t, p, 0], vg_recv_sem.at[t, p, 0], left),
            remote(vg_send.at[t, p, 1], vg_recv.at[t, p, 0], vg_send_sem.at[t, p, 1], vg_recv_sem.at[t, p, 1], right),
        ]

    def advance(t, p):
        moving = is_moving(t)
        pieces = []
        square = None
        place_tiles = []
        for d in range(3):
            half = state_v[p, d] + (0.5 * step_time) * state_g[p, d]
            x = state_x[p, d] + (moving * step_time) * half
            state_v[p, d] = half
            state_x[p, d] = x
            x = x - middle[d]
            place_tiles.append([x[:, at:at + LANES] for at in range(0, wide, LANES)])
            square = x * x if square is None else square + x * x
            pieces.append(thirds(x))
        stack = [piece for three in pieces for piece in three]
        stack += [piece for three in pieces for piece in (three[0], three[0], three[1])]
        stack += thirds(square)
        stack += [jnp.ones((SPLITS * group, wide), F32), jnp.zeros((LANES - TERMS * group, wide), F32)]
        tall = jnp.concatenate(stack, axis=0)
        for at in range(0, wide, LANES):
            cols[p, at:at + LANES, :] = tall[:, at:at + LANES].T.astype(BF16)
        for d in range(3):
            xb[p, d] = jnp.dot(cols[p, 0:ext * NA, :], selector[d], preferred_element_type=F32)
        def stage(i):
            count = near // CHUNK

            def some(begin, end):
                if i < inner:
                    pairs(p, i, count * begin // 12, count * end // 12)

            hidden = revise(p, i - 2) if i >= 2 else None
            some(0, 1)
            if 1 <= i <= inner:
                gather_scalar(p, i - 1, [functools.partial(some, *span) for span in ((1, 2), (2, 3), (3, 4), (4, 5), (5, 6), (6, 6))])
            else:
                some(1, 6)
            if i + 1 < inner:
                weigh(p, i + 1, place_tiles)
                measure(p, i + 1)
            some(6, 7)
            if i >= 2:
                read(p, i - 2, hidden)
            some(7, 8)
            if 1 <= i <= inner:
                gather_vector(p, i - 1, [functools.partial(some, *span) for span in ((8, 9), (9, 10), (10, 11))])
            else:
                some(8, 11)
            some(11, 12)

        weigh(p, 0, place_tiles)
        measure(p, 0)
        stage(0)
        for i in range(1, inner - 1):
            pl.when(lax.rem((me + i) * (me + i + 1), 2) < 1)(functools.partial(stage, i))
        stage(inner - 1)
        empty = [lambda: None] * 3
        gather_scalar(p, inner - 1, empty[:1])
        hidden = revise(p, inner - 2)
        gather_vector(p, inner - 1, empty)
        read(p, inner - 2, hidden)
        for i in range(1, inner - 3):
            force(p, i)
        hidden = revise(p, inner - 1)
        for i in range(max(1, inner - 3), inner - 2):
            force(p, i)
        read(p, inner - 1, hidden)
        force(p, inner - 2)
        kinetic = jnp.zeros((group, 1), F32)
        for d in range(3):
            joined = []
            for c in range(0, cells, 2):
                even = pushes[p, c + 1, d]
                odd = pushes[p, c + 2, d] if c + 1 < cells else jnp.zeros((group, LANES), F32)
                joined.append(jnp.where(half_lane, even, odd))
            g = jnp.concatenate(joined, axis=1)[:, :own]
            v = state_v[p, d, :, edge:edge + own] + (moving * (0.5 * step_time)) * g
            vg_send[t, p, 0, d] = jnp.concatenate([v[:, :edge], g[:, :edge]], axis=1)
            vg_send[t, p, 1, d] = jnp.concatenate([v[:, own - edge:], g[:, own - edge:]], axis=1)
            kinetic = kinetic + jnp.sum(v * v, axis=1, keepdims=True)
            state_v[p, d, :, edge:edge + own] = v
            state_g[p, d, :, edge:edge + own] = g
        across = jnp.sum(jnp.where(diagonal, kinetic, 0.0), axis=0, keepdims=True)
        kin_send[t, p] = across
        kin_recv[t, p, n - 1] = across

        def spread(d, inner_carry):
            remote(
                kin_send.at[t, p], kin_recv.at[t, p, d - 1], kin_send_sem.at[t, p],
                kin_recv_sem.at[t, p], lax.rem(me + d, n),
            ).start()
            return inner_carry

        for copy in vg_copies(t, p):
            copy.start()
        if n <= 16:
            for d in sorted(range(1, n), key=lambda d: min(d, n - d)):
                spread(d, 0)
        else:
            lax.fori_loop(1, n, spread, 0)

    def finish(t, p):
        everything = kin_recv.at[t, p, pl.ds(0, n - 1)]
        for copy in vg_copies(t, p):
            copy.wait()
        pltpu.make_async_copy(everything, everything, kin_send_sem.at[t, p]).wait()
        pltpu.make_async_copy(everything, everything, kin_recv_sem.at[t, p]).wait()
        collected = jnp.sum(kin_recv[t, p], axis=0)
        gathered = jnp.sum(jnp.where(diagonal, collected, 0.0), axis=1, keepdims=True)
        goal = target[p * group:(p + 1) * group]
        stretch = jnp.sqrt(goal / (gathered / (3.0 * own * n) + motion_work_lower_limit))
        stretch = jnp.where(t > 0, stretch, 1.0)
        rest = jnp.zeros((group, wide - ext * NA), F32)
        for d in range(3):
            from_left, from_right = vg_recv[t, p, 0, d], vg_recv[t, p, 1, d]
            state_v[p, d] = stretch * jnp.concatenate(
                [from_left[:, :edge], state_v[p, d, :, edge:edge + own], from_right[:, :edge], rest], axis=1
            )
            state_g[p, d, :, 0:edge] = from_left[:, edge:]
            state_g[p, d, :, edge + own:2 * edge + own] = from_right[:, edge:]

    def step(t, carry):
        for p in range(parts):
            pl.when(t > 0)(functools.partial(finish, t - 1, p))
            advance(t, p)
        return carry

    lax.fori_loop(0, STEPS + 1, step, 0)
    for p in range(parts):
        finish(STEPS, p)

    def pick(values):
        result = jnp.zeros_like(values)
        for r in range(replicas):
            result = jnp.where(source == r, values[r:r + 1], result)
        return result

    def whole(state, d):
        return jnp.concatenate([state[p, d, :, edge:edge + own] for p in range(parts)], axis=0)

    heat = jnp.sqrt(target / pick(target))
    floor = (lax.broadcasted_iota(jnp.int32, (1, own), 1) // NA).astype(F32)
    for d in range(3):
        x = pick(whole(state_x, d))
        if d == 2:
            x = x - floor
        places_out[d] = x
        speeds_out[d] = pick(whole(state_v, d)) * heat
        forces_out[d] = pick(whole(state_g, d))


def on_device(
    particle_places,
    particle_speeds,
    thermal_targets,
    element_features,
    swap_counterpart_slot,
    swap_approval_flags,
    initial_signal_projector,
    initial_distance_filter,
    initial_directional_scales,
    invariant_revision_matrix,
    magnitude_revision_matrix,
    later_signal_projector,
    later_directional_scales,
    push_output_matrix,
):
    n = lax.axis_size("dom")
    replicas, _, own = particle_places.shape
    cells = own // NA
    channels = element_features.shape[1]
    ext = cells + 2 * HALO
    inner = cells + 2
    edge = HALO * NA
    wide = -(-ext * NA // LANES) * LANES
    rounds = STEPS + 1
    group = 4
    parts = replicas // group
    lanes = group * NA
    basis = initial_distance_filter.shape[0]
    depth = basis * 3 * NA
    vmem = pl.BlockSpec(memory_space=pltpu.VMEM)
    smem = pl.BlockSpec(memory_space=pltpu.SMEM)
    outside = pl.BlockSpec(memory_space=pl.ANY)
    out = jax.ShapeDtypeStruct((3, replicas, own), F32)
    results = pl.pallas_call(
        functools.partial(kernel, n, replicas, cells, parts),
        out_shape=(out, out, out),
        in_specs=[outside, outside, smem, smem, smem] + [outside] * 9,
        out_specs=(vmem, vmem, vmem),
        scratch_shapes=[
            pltpu.VMEM((3, replicas, own), F32),
            pltpu.VMEM((3, replicas, own), F32),
            pltpu.VMEM((wide, channels), BF16),
            pltpu.VMEM((channels, channels), BF16),
            pltpu.VMEM((basis, channels), F32),
            pltpu.VMEM((1, channels), F32),
            pltpu.VMEM((channels, channels), BF16),
            pltpu.VMEM((channels, channels), BF16),
            pltpu.VMEM((channels, channels), BF16),
            pltpu.VMEM((1, channels), F32),
            pltpu.VMEM((1, channels), F32),
            pltpu.VMEM((2, 3, replicas, own), F32),
            pltpu.VMEM((inner, channels, depth), BF16),
            pltpu.VMEM((inner, channels, 4 * NA), BF16),
            pltpu.VMEM((inner, channels, LANES), F32),
            pltpu.VMEM((channels, 2 * channels), BF16),
            pltpu.VMEM((channels, LANES), F32),
            pltpu.VMEM((16, channels), BF16),
            pltpu.VMEM((1, wide + LANES), F32),
            pltpu.VMEM((3, LANES, lanes), BF16),
            pltpu.VMEM((parts, 3, group, wide), F32),
            pltpu.VMEM((parts, 3, group, wide), F32),
            pltpu.VMEM((parts, 3, group, wide), F32),
            pltpu.VMEM((parts, wide, LANES), BF16),
            pltpu.VMEM((parts, 3, ext * NA, lanes), F32),
            pltpu.VMEM((parts, inner, 3, 8, lanes), F32),
            pltpu.VMEM((parts, inner, LANES, lanes), BF16),
            pltpu.VMEM((parts, inner, 3 * NA, lanes), F32),
            pltpu.VMEM((parts, inner, depth, lanes), BF16),
            pltpu.VMEM((parts, inner, 3, 4 * NA, lanes), BF16),
            pltpu.VMEM((parts, inner, 2 * channels, lanes), BF16),
            pltpu.VMEM((parts, inner, 8, lanes), F32),
            pltpu.VMEM((parts, inner, 3, group, LANES), F32),
            pltpu.VMEM((rounds, parts, 2, 3, group, 2 * edge), F32),
            pltpu.VMEM((rounds, parts, 2, 3, group, 2 * edge), F32),
            pltpu.VMEM((rounds, parts, 1, LANES), F32),
            pltpu.VMEM((rounds, parts, n, 1, LANES), F32),
            pltpu.SemaphoreType.DMA((11,)),
            pltpu.SemaphoreType.DMA((4,)),
            pltpu.SemaphoreType.DMA((4,)),
            pltpu.SemaphoreType.DMA((rounds, parts, 2)),
            pltpu.SemaphoreType.DMA((rounds, parts, 2)),
            pltpu.SemaphoreType.DMA((rounds, parts)),
            pltpu.SemaphoreType.DMA((rounds, parts)),
        ],
        compiler_params=pltpu.CompilerParams(
            collective_id=0, has_side_effects=True, vmem_limit_bytes=63 * 1024 * 1024
        ),
    )(
        jnp.transpose(particle_places, (1, 0, 2)),
        jnp.transpose(particle_speeds, (1, 0, 2)),
        thermal_targets,
        swap_counterpart_slot,
        swap_approval_flags,
        element_features,
        initial_signal_projector,
        initial_distance_filter,
        initial_directional_scales.reshape(1, -1),
        invariant_revision_matrix,
        magnitude_revision_matrix,
        later_signal_projector,
        later_directional_scales.reshape(1, -1),
        push_output_matrix.reshape(1, -1),
    )
    return tuple(jnp.transpose(result, (1, 0, 2)) for result in results)
def solution(mesh):
    along = P("groups", None, "dom")
    return jax.shard_map(
        on_device,
        mesh=mesh,
        in_specs=(
            along,
            along,
            P("groups"),
            P(("groups", "dom"), None),
            P("groups"),
            P("groups"),
            P(),
            P(),
            P(),
            P(),
            P(),
            P(),
            P(),
            P(),
        ),
        out_specs=(along, along, along),
        check_vma=False,
    )
```

```python
import functools
import math

import jax
import jax.numpy as jnp
from jax import lax
from jax.experimental import pallas as pl
from jax.experimental.pallas import tpu as pltpu
from jax.sharding import PartitionSpec as P

NA = 64
STEPS = 4
LANES = 128
CHUNK = 16
HALO = 2
SPLITS = 3
TERMS = 24
LOG2E = math.log2(math.e)

step_time = 0.05
motion_work_lower_limit = 1e-06

F32 = jnp.float32
BF16 = jnp.bfloat16
MESH = pl.DeviceIdType.MESH


def split_bf16(values):
    high = values.astype(BF16)
    low = (values - high.astype(F32)).astype(BF16)
    return high, low


def weight_rows(weights):
    high, low = split_bf16(weights)
    high, low = high.astype(F32), low.astype(F32)
    row = lax.broadcasted_iota(jnp.int32, (16, weights.shape[1]), 0)
    return jnp.where(row == 0, high, jnp.where(row == 1, low, 0.0)).astype(BF16)


def swap_halves(values):
    return pltpu.roll(values, NA, 1)


def kernel(
    n, replicas, cells, parts,
    places, speeds, targets, slots, flags, features,
    projector, radial_filter, scales_one, invariant, magnitude, later_projector, scales_two, push,
    places_out, speeds_out, forces_out,
    own_places, own_speeds, feats, w_project, w_filter, w_scale_one, w_invariant, w_magnitude,
    w_later, w_scale_two, w_push,
    place_halo, table_one, table_vec, feat_t, mix, read_two, s_one, selector,
    state_x, state_v, state_g, cols, xb, mine, near_w, apart, gauss, vecs, mixed, flats, pushes,
    vg_send, vg_recv, kin_send, kin_recv,
    load_sem, init_send_sem, init_recv_sem, vg_send_sem, vg_recv_sem, kin_send_sem, kin_recv_sem,
):
    me = lax.axis_index("dom")
    left = lax.rem(me + n - 1, n)
    right = lax.rem(me + 1, n)
    own = cells * NA
    edge = HALO * NA
    ext = cells + 2 * HALO
    inner = cells + 2
    wide = state_x.shape[3]
    group = replicas // parts
    lanes = group * NA
    tiles = lanes // LANES
    channels = features.shape[1]
    basis = radial_filter.shape[0]
    near = 3 * NA

    barrier = pltpu.get_barrier_semaphore()

    def greet(d, carry):
        pl.semaphore_signal(barrier, inc=1, device_id={"dom": lax.rem(me + d, n)}, device_id_type=MESH)
        return carry

    loads = [
        (features, feats.at[pl.ds(edge, own)]),
        (projector, w_project),
        (places, own_places),
        (speeds, own_speeds),
        (radial_filter, w_filter),
        (scales_one, w_scale_one),
        (invariant, w_invariant),
        (magnitude, w_magnitude),
        (later_projector, w_later),
        (scales_two, w_scale_two),
        (push, w_push),
    ]
    loads = [pltpu.make_async_copy(src, dst, load_sem.at[i]) for i, (src, dst) in enumerate(loads)]
    for load in loads:
        load.start()
    lax.fori_loop(1, n, greet, 0)

    def remote(src, dst, send_sem, recv_sem, to):
        return pltpu.make_async_remote_copy(
            src_ref=src, dst_ref=dst, send_sem=send_sem, recv_sem=recv_sem,
            device_id={"dom": to}, device_id_type=MESH,
        )

    first = [
        remote(places, place_halo.at[1], init_send_sem.at[0], init_recv_sem.at[0], left),
        remote(places, place_halo.at[0], init_send_sem.at[1], init_recv_sem.at[1], right),
        remote(
            features.at[pl.ds(0, edge)], feats.at[pl.ds(edge + own, edge)],
            init_send_sem.at[2], init_recv_sem.at[2], left,
        ),
        remote(
            features.at[pl.ds(own - edge, edge)], feats.at[pl.ds(0, edge)],
            init_send_sem.at[3], init_recv_sem.at[3], right,
        ),
    ]
    pl.semaphore_wait(barrier, n - 1)
    for copy in first:
        copy.start()
    for load in loads:
        load.wait()

    half_lane = lax.broadcasted_iota(jnp.int32, (1, LANES), 1) < NA
    member_row = lax.broadcasted_iota(jnp.int32, (group, 1), 0)

    def flip(values):
        return values.astype(F32).T

    offset = lax.broadcasted_iota(jnp.int32, (basis, channels), 0).astype(F32) - 0.5 * (basis - 1)
    filters = (w_filter[...] * jnp.exp(-2.0 * offset * offset)).T
    push_row = w_push[...]
    w_one = weight_rows(w_scale_one[...] * push_row)
    back = lax.dot_general(
        weight_rows(w_scale_two[...] * push_row), w_later[...], (((1,), (1,)), ((), ())),
        preferred_element_type=F32,
    )
    read_two[...] = weight_rows(back[0:1] + back[1:2])
    mix[:, 0:channels] = (0.5 * flip(w_invariant[...])).astype(BF16)
    scale_row = w_scale_one[...] * w_scale_one[...]
    mix[:, channels:2 * channels] = (0.5 * flip(w_magnitude[...]) * scale_row).astype(BF16)

    k_row = lax.broadcasted_iota(jnp.int32, (LANES, lanes), 0)
    k_lane = lax.broadcasted_iota(jnp.int32, (LANES, lanes), 1)
    for d in range(3):
        base = d * SPLITS * group
        inside = (k_row >= base) & (k_row < base + SPLITS * group)
        chosen = inside & ((k_row - base) % group == k_lane // NA)
        selector[d] = jnp.where(chosen, 1.0, 0.0).astype(BF16)
    for p in range(parts):
        for i in range(inner):
            for d in range(3):
                vecs[p, i, d, near:, :] = jnp.zeros((4 * NA - near, lanes), BF16)
            near_w[p, i, TERMS * group:, :] = jnp.zeros((LANES - TERMS * group, lanes), BF16)
    feats[ext * NA:, :] = jnp.zeros((wide - ext * NA, channels), BF16)

    total = cells * n
    floor_own = (me * cells).astype(F32)
    floor_left = (me * cells + jnp.where(me == 0, total, 0)).astype(F32)
    floor_right = (me * cells - jnp.where(me == n - 1, total, 0)).astype(F32)
    lift = [0.0, 0.0, 1.0]
    tail = jnp.zeros((group, wide - ext * NA), F32)
    for p in range(parts):
        members = slice(p * group, (p + 1) * group)
        for d in range(3):
            state_v[p, d] = jnp.concatenate(
                [jnp.zeros((group, edge), F32), own_speeds[d, members, :], jnp.zeros((group, edge), F32), tail],
                axis=1,
            )
            state_g[p, d] = jnp.zeros((group, wide), F32)

    for copy in first:
        copy.wait()

    for p in range(parts):
        members = slice(p * group, (p + 1) * group)
        for d in range(3):
            state_x[p, d] = jnp.concatenate(
                [
                    place_halo[0, d, members, own - edge:] - lift[d] * floor_left,
                    own_places[d, members, :] - lift[d] * floor_own,
                    place_halo[1, d, members, :edge] - lift[d] * floor_right,
                    tail,
                ],
                axis=1,
            )

    signals = jnp.dot(feats[...], w_project[...], preferred_element_type=F32).astype(BF16)
    signal_tiles = [flip(signals[at:at + LANES]) for at in range(0, wide, LANES)]
    feat_tiles = [flip(feats[at:at + LANES, :]) for at in range(0, wide, LANES)]

    def double(tile_list, e):
        tile = tile_list[e // 2]
        other = swap_halves(tile)
        return jnp.where(half_lane, tile, other) if e % 2 == 0 else jnp.where(half_lane, other, tile)

    doubles = [double(signal_tiles, e) for e in range(ext)]
    flat_signals = jnp.concatenate(signal_tiles, axis=1).astype(BF16)
    out = jnp.dot(w_one, flat_signals, preferred_element_type=F32)
    s_one[:, 0:wide] = out[0:1] + out[1:2]
    s_one[:, wide:] = jnp.zeros((1, LANES), F32)
    for i in range(inner):
        feat_t[i] = double(feat_tiles, i + 1)
        pair = jnp.where(half_lane, doubles[i], doubles[i + 1])
        table_vec[i, :, 0:LANES] = pair.astype(BF16)
        table_vec[i, :, LANES:2 * LANES] = jnp.where(half_lane, doubles[i + 2], 0.0).astype(BF16)
        for k in range(basis):
            col = jnp.broadcast_to(filters[:, k:k + 1], (channels, LANES))
            table_one[i, :, k * LANES:(k + 1) * LANES] = (pair * col).astype(BF16)
            if k % 2 == 1:
                both = jnp.where(half_lane, jnp.broadcast_to(filters[:, k - 1:k], (channels, LANES)), col)
                at = basis * LANES + (k // 2) * LANES
                table_one[i, :, at:at + LANES] = (doubles[i + 2] * both).astype(BF16)

    replica_row = lax.broadcasted_iota(jnp.int32, (replicas, 1), 0)
    diagonal = (
        lax.broadcasted_iota(jnp.int32, (group, LANES), 0)
        == lax.broadcasted_iota(jnp.int32, (group, LANES), 1)
    )
    target = jnp.zeros((replicas, 1), F32)
    source = jnp.zeros((replicas, 1), jnp.int32)
    for r in range(replicas):
        target = jnp.where(replica_row == r, targets[r], target)
        source = jnp.where(replica_row == r, jnp.where(flags[r] > 0, slots[r], r), source)

    def spread_row(tile_list, e):
        tile = tile_list[e // 2]
        other = swap_halves(tile)
        first_half, second_half = (tile, other) if e % 2 == 0 else (other, tile)
        return [
            jnp.where(half_lane, first_half[2 * m:2 * m + 1], second_half[2 * m + 1:2 * m + 2])
            for m in range(tiles)
        ]

    def thirds(values):
        result = []
        for s in range(SPLITS):
            piece = values.astype(BF16).astype(F32)
            values = values - piece
            result.append(piece)
        return result

    middle = [0.5, 0.5, 0.5 * cells]
    eight_row = lax.broadcasted_iota(jnp.int32, (2 * group, lanes), 0)
    upper = eight_row < group
    own_lane = eight_row % group == lax.broadcasted_iota(jnp.int32, (2 * group, lanes), 1) // NA

    def gather_rows(values, odd):
        result = None
        for r in range(group):
            tile = values[:, (r // 2) * LANES:(r // 2 + 1) * LANES]
            if (r % 2 == 1) != odd:
                tile = swap_halves(tile)
            result = tile if result is None else jnp.where(member_row == r, tile, result)
        return jnp.broadcast_to(result, (group, LANES))

    def weigh(p, i, place_tiles):
        rows = []
        left_over = None
        for d in range(3):
            spread = jnp.concatenate(spread_row(place_tiles[d], i + 1), axis=1)
            mine[p, i, d] = jnp.broadcast_to(spread, (8, lanes))
            left_over = 1.0 - spread * spread if left_over is None else left_over - spread * spread
            rows.append(thirds(2.0 * spread))
        terms = [three[0] for three in rows for _ in range(SPLITS)]
        terms += [piece for three in rows for piece in (three[1], three[2], three[1])]
        terms += [jnp.full((1, lanes), -1.0, F32)] * SPLITS + thirds(left_over)
        for at in range(0, TERMS, 4):
            block = jnp.concatenate(
                [
                    jnp.where(own_lane, jnp.where(upper, terms[m], terms[m + 1]), 0.0)
                    for m in (at, at + 2)
                ],
                axis=0,
            )
            near_w[p, i, at * group:(at + 4) * group, :] = block.astype(BF16)

    def measure(p, i):
        window = cols[p, i * NA:i * NA + near, :]
        apart[p, i] = jnp.dot(window, near_w[p, i], preferred_element_type=F32)

    def pairs(p, i, begin, end):
        mine_now = [jnp.concatenate([mine[p, i, d]] * (CHUNK // 8), axis=0) for d in range(3)]
        for at in range(begin * CHUNK, end * CHUNK, CHUNK):
            row = i * NA + at
            inside = jnp.maximum(apart[p, i, at:at + CHUNK, :], 0.0)
            envelope = inside * inside
            for d in range(3):
                step = xb[p, d, row:row + CHUNK, :] - mine_now[d]
                vecs[p, i, d, at:at + CHUNK, :] = (step * envelope).astype(BF16)
            centered = 0.5 - inside
            power = (centered * (centered - 1.0 / (basis - 1))) * (-98.0 * LOG2E)
            start = (jnp.exp2(power) * envelope).astype(BF16)
            grow = jnp.exp2(centered * (28.0 * LOG2E)).astype(BF16)
            shrink = jnp.exp2(centered * (-28.0 * LOG2E)).astype(BF16)
            values = {basis // 2: start}
            for k in range(basis // 2, basis - 1):
                values[k + 1] = values[k] * grow
            for k in range(basis // 2, 0, -1):
                values[k - 1] = values[k] * shrink
            for k in range(basis):
                if at < 2 * NA:
                    to = k * LANES + at
                else:
                    to = basis * LANES + k * NA + at - 2 * NA
                gauss[p, i, to:to + CHUNK, :] = values[k]

    def gather_scalar(p, i, between):
        depth = table_one.shape[2] // len(between)
        scalar = None
        for m, fill in enumerate(between):
            part = slice(m * depth, (m + 1) * depth)
            term = jnp.dot(table_one[i, :, part], gauss[p, i, part, :], preferred_element_type=F32)
            scalar = term if scalar is None else scalar + term
            fill()
        mixed[p, i, 0:channels, :] = scalar.astype(BF16)

    def gather_vector(p, i, between):
        norm = None
        for d in range(3):
            vec = jnp.dot(table_vec[i], vecs[p, i, d], preferred_element_type=F32)
            norm = vec * vec if norm is None else norm + vec * vec
            between[d]()
        mixed[p, i, channels:, :] = norm.astype(BF16)

    def revise(p, i):
        half = jnp.dot(mix[...], mixed[p, i], preferred_element_type=F32)
        hidden = half * jnp.tanh(half) + half + jnp.concatenate([feat_t[i]] * tiles, axis=1)
        return hidden.astype(BF16)

    def read(p, i, hidden):
        out = jnp.dot(read_two[...], hidden, preferred_element_type=F32)
        flats[p, i] = jnp.broadcast_to(out[0:1] + out[1:2], (8, lanes))

    def force(p, i):
        even, odd, last = [
            gather_rows(flats[p, i + j, 0:1, :], odd) for j, odd in ((-1, False), (0, True), (1, False))
        ]
        window = jnp.concatenate([jnp.where(half_lane, even, odd), jnp.where(half_lane, last, 0.0)], axis=1)
        window = window + s_one[:, i * NA:(i + 4) * NA]
        high, low = split_bf16(window)
        stacked = jnp.concatenate([high.astype(F32), low.astype(F32)], axis=0)
        stacked = jnp.concatenate([stacked] * (16 // (2 * group)), axis=0).astype(BF16)
        for d in range(3):
            out = jnp.dot(stacked, vecs[p, i, d], preferred_element_type=F32)
            pushes[p, i, d] = gather_rows(out[:group] + out[group:2 * group], i % 2 == 0)

    def is_moving(t):
        return jnp.where(t > 0, 1.0, 0.0).astype(F32)

    def vg_copies(t, p):
        return [
            remote(vg_send.at[t, p, 0], vg_recv.at[t, p, 1], vg_send_sem.at[t, p, 0], vg_recv_sem.at[t, p, 0], left),
            remote(vg_send.at[t, p, 1], vg_recv.at[t, p, 0], vg_send_sem.at[t, p, 1], vg_recv_sem.at[t, p, 1], right),
        ]

    def advance(t, p):
        moving = is_moving(t)
        pieces = []
        square = None
        place_tiles = []
        for d in range(3):
            half = state_v[p, d] + (0.5 * step_time) * state_g[p, d]
            x = state_x[p, d] + (moving * step_time) * half
            state_v[p, d] = half
            state_x[p, d] = x
            x = x - middle[d]
            place_tiles.append([x[:, at:at + LANES] for at in range(0, wide, LANES)])
            square = x * x if square is None else square + x * x
            pieces.append(thirds(x))
        stack = [piece for three in pieces for piece in three]
        stack += [piece for three in pieces for piece in (three[0], three[0], three[1])]
        stack += thirds(square)
        stack += [jnp.ones((SPLITS * group, wide), F32), jnp.zeros((LANES - TERMS * group, wide), F32)]
        tall = jnp.concatenate(stack, axis=0)
        for at in range(0, wide, LANES):
            cols[p, at:at + LANES, :] = tall[:, at:at + LANES].T.astype(BF16)
        for d in range(3):
            xb[p, d] = jnp.dot(cols[p, 0:ext * NA, :], selector[d], preferred_element_type=F32)
        def stage(i):
            count = near // CHUNK

            def some(begin, end):
                if i < inner:
                    pairs(p, i, count * begin // 12, count * end // 12)

            hidden = revise(p, i - 2) if i >= 2 else None
            some(0, 1)
            if 1 <= i <= inner:
                gather_scalar(p, i - 1, [functools.partial(some, *span) for span in ((1, 2), (2, 3), (3, 4), (4, 5), (5, 6), (6, 6))])
            else:
                some(1, 6)
            if i + 1 < inner:
                weigh(p, i + 1, place_tiles)
                measure(p, i + 1)
            some(6, 7)
            if i >= 2:
                read(p, i - 2, hidden)
            some(7, 8)
            if 1 <= i <= inner:
                gather_vector(p, i - 1, [functools.partial(some, *span) for span in ((8, 9), (9, 10), (10, 11))])
            else:
                some(8, 11)
            some(11, 12)

        weigh(p, 0, place_tiles)
        measure(p, 0)
        stage(0)
        for i in range(1, inner - 1):
            pl.when(lax.rem((me + i) * (me + i + 1), 2) < 1)(functools.partial(stage, i))
        stage(inner - 1)
        empty = [lambda: None] * 3
        gather_scalar(p, inner - 1, empty[:1])
        hidden = revise(p, inner - 2)
        gather_vector(p, inner - 1, empty)
        read(p, inner - 2, hidden)
        for i in range(1, inner - 3):
            force(p, i)
        hidden = revise(p, inner - 1)
        for i in range(max(1, inner - 3), inner - 2):
            force(p, i)
        read(p, inner - 1, hidden)
        force(p, inner - 2)
        kinetic = jnp.zeros((group, 1), F32)
        for d in range(3):
            joined = []
            for c in range(0, cells, 2):
                even = pushes[p, c + 1, d]
                odd = pushes[p, c + 2, d] if c + 1 < cells else jnp.zeros((group, LANES), F32)
                joined.append(jnp.where(half_lane, even, odd))
            g = jnp.concatenate(joined, axis=1)[:, :own]
            v = state_v[p, d, :, edge:edge + own] + (moving * (0.5 * step_time)) * g
            vg_send[t, p, 0, d] = jnp.concatenate([v[:, :edge], g[:, :edge]], axis=1)
            vg_send[t, p, 1, d] = jnp.concatenate([v[:, own - edge:], g[:, own - edge:]], axis=1)
            kinetic = kinetic + jnp.sum(v * v, axis=1, keepdims=True)
            state_v[p, d, :, edge:edge + own] = v
            state_g[p, d, :, edge:edge + own] = g
        across = jnp.sum(jnp.where(diagonal, kinetic, 0.0), axis=0, keepdims=True)
        kin_send[t, p] = across
        kin_recv[t, p, n - 1] = across

        def spread(d, inner_carry):
            remote(
                kin_send.at[t, p], kin_recv.at[t, p, d - 1], kin_send_sem.at[t, p],
                kin_recv_sem.at[t, p], lax.rem(me + d, n),
            ).start()
            return inner_carry

        for copy in vg_copies(t, p):
            copy.start()
        if n <= 16:
            for d in sorted(range(1, n), key=lambda d: min(d, n - d)):
                spread(d, 0)
        else:
            lax.fori_loop(1, n, spread, 0)

    def finish(t, p):
        everything = kin_recv.at[t, p, pl.ds(0, n - 1)]
        for copy in vg_copies(t, p):
            copy.wait()
        pltpu.make_async_copy(everything, everything, kin_send_sem.at[t, p]).wait()
        pltpu.make_async_copy(everything, everything, kin_recv_sem.at[t, p]).wait()
        collected = jnp.sum(kin_recv[t, p], axis=0)
        gathered = jnp.sum(jnp.where(diagonal, collected, 0.0), axis=1, keepdims=True)
        goal = target[p * group:(p + 1) * group]
        stretch = jnp.sqrt(goal / (gathered / (3.0 * own * n) + motion_work_lower_limit))
        stretch = jnp.where(t > 0, stretch, 1.0)
        rest = jnp.zeros((group, wide - ext * NA), F32)
        for d in range(3):
            from_left, from_right = vg_recv[t, p, 0, d], vg_recv[t, p, 1, d]
            state_v[p, d] = stretch * jnp.concatenate(
                [from_left[:, :edge], state_v[p, d, :, edge:edge + own], from_right[:, :edge], rest], axis=1
            )
            state_g[p, d, :, 0:edge] = from_left[:, edge:]
            state_g[p, d, :, edge + own:2 * edge + own] = from_right[:, edge:]

    def step(t, carry):
        for p in range(parts):
            pl.when(t > 0)(functools.partial(finish, t - 1, p))
            advance(t, p)
        return carry

    lax.fori_loop(0, STEPS + 1, step, 0)
    for p in range(parts):
        finish(STEPS, p)

    def pick(values):
        result = jnp.zeros_like(values)
        for r in range(replicas):
            result = jnp.where(source == r, values[r:r + 1], result)
        return result

    def whole(state, d):
        return jnp.concatenate([state[p, d, :, edge:edge + own] for p in range(parts)], axis=0)

    heat = jnp.sqrt(target / pick(target))
    floor = (lax.broadcasted_iota(jnp.int32, (1, own), 1) // NA).astype(F32)
    for d in range(3):
        x = pick(whole(state_x, d))
        if d == 2:
            x = x - floor
        places_out[d] = x
        speeds_out[d] = pick(whole(state_v, d)) * heat
        forces_out[d] = pick(whole(state_g, d))


def on_device(
    particle_places,
    particle_speeds,
    thermal_targets,
    element_features,
    swap_counterpart_slot,
    swap_approval_flags,
    initial_signal_projector,
    initial_distance_filter,
    initial_directional_scales,
    invariant_revision_matrix,
    magnitude_revision_matrix,
    later_signal_projector,
    later_directional_scales,
    push_output_matrix,
):
    n = lax.axis_size("dom")
    replicas, _, own = particle_places.shape
    cells = own // NA
    channels = element_features.shape[1]
    ext = cells + 2 * HALO
    inner = cells + 2
    edge = HALO * NA
    wide = -(-ext * NA // LANES) * LANES
    rounds = STEPS + 1
    group = 4
    parts = replicas // group
    lanes = group * NA
    basis = initial_distance_filter.shape[0]
    depth = basis * 3 * NA
    vmem = pl.BlockSpec(memory_space=pltpu.VMEM)
    smem = pl.BlockSpec(memory_space=pltpu.SMEM)
    outside = pl.BlockSpec(memory_space=pl.ANY)
    out = jax.ShapeDtypeStruct((3, replicas, own), F32)
    results = pl.pallas_call(
        functools.partial(kernel, n, replicas, cells, parts),
        out_shape=(out, out, out),
        in_specs=[outside, outside, smem, smem, smem] + [outside] * 9,
        out_specs=(vmem, vmem, vmem),
        scratch_shapes=[
            pltpu.VMEM((3, replicas, own), F32),
            pltpu.VMEM((3, replicas, own), F32),
            pltpu.VMEM((wide, channels), BF16),
            pltpu.VMEM((channels, channels), BF16),
            pltpu.VMEM((basis, channels), F32),
            pltpu.VMEM((1, channels), F32),
            pltpu.VMEM((channels, channels), BF16),
            pltpu.VMEM((channels, channels), BF16),
            pltpu.VMEM((channels, channels), BF16),
            pltpu.VMEM((1, channels), F32),
            pltpu.VMEM((1, channels), F32),
            pltpu.VMEM((2, 3, replicas, own), F32),
            pltpu.VMEM((inner, channels, depth), BF16),
            pltpu.VMEM((inner, channels, 4 * NA), BF16),
            pltpu.VMEM((inner, channels, LANES), F32),
            pltpu.VMEM((channels, 2 * channels), BF16),
            pltpu.VMEM((16, channels), BF16),
            pltpu.VMEM((1, wide + LANES), F32),
            pltpu.VMEM((3, LANES, lanes), BF16),
            pltpu.VMEM((parts, 3, group, wide), F32),
            pltpu.VMEM((parts, 3, group, wide), F32),
            pltpu.VMEM((parts, 3, group, wide), F32),
            pltpu.VMEM((parts, wide, LANES), BF16),
            pltpu.VMEM((parts, 3, ext * NA, lanes), F32),
            pltpu.VMEM((parts, inner, 3, 8, lanes), F32),
            pltpu.VMEM((parts, inner, LANES, lanes), BF16),
            pltpu.VMEM((parts, inner, 3 * NA, lanes), F32),
            pltpu.VMEM((parts, inner, depth, lanes), BF16),
            pltpu.VMEM((parts, inner, 3, 4 * NA, lanes), BF16),
            pltpu.VMEM((parts, inner, 2 * channels, lanes), BF16),
            pltpu.VMEM((parts, inner, 8, lanes), F32),
            pltpu.VMEM((parts, inner, 3, group, LANES), F32),
            pltpu.VMEM((rounds, parts, 2, 3, group, 2 * edge), F32),
            pltpu.VMEM((rounds, parts, 2, 3, group, 2 * edge), F32),
            pltpu.VMEM((rounds, parts, 1, LANES), F32),
            pltpu.VMEM((rounds, parts, n, 1, LANES), F32),
            pltpu.SemaphoreType.DMA((11,)),
            pltpu.SemaphoreType.DMA((4,)),
            pltpu.SemaphoreType.DMA((4,)),
            pltpu.SemaphoreType.DMA((rounds, parts, 2)),
            pltpu.SemaphoreType.DMA((rounds, parts, 2)),
            pltpu.SemaphoreType.DMA((rounds, parts)),
            pltpu.SemaphoreType.DMA((rounds, parts)),
        ],
        compiler_params=pltpu.CompilerParams(
            collective_id=0, has_side_effects=True, vmem_limit_bytes=63 * 1024 * 1024
        ),
    )(
        jnp.transpose(particle_places, (1, 0, 2)),
        jnp.transpose(particle_speeds, (1, 0, 2)),
        thermal_targets,
        swap_counterpart_slot,
        swap_approval_flags,
        element_features,
        initial_signal_projector,
        initial_distance_filter,
        initial_directional_scales.reshape(1, -1),
        invariant_revision_matrix,
        magnitude_revision_matrix,
        later_signal_projector,
        later_directional_scales.reshape(1, -1),
        push_output_matrix.reshape(1, -1),
    )
    return tuple(jnp.transpose(result, (1, 0, 2)) for result in results)
def solution(mesh):
    along = P("groups", None, "dom")
    return jax.shard_map(
        on_device,
        mesh=mesh,
        in_specs=(
            along,
            along,
            P("groups"),
            P(("groups", "dom"), None),
            P("groups"),
            P("groups"),
            P(),
            P(),
            P(),
            P(),
            P(),
            P(),
            P(),
            P(),
        ),
        out_specs=(along, along, along),
        check_vma=False,
    )
```
